32 devices in a mesh: gx: 8 (over y, x, core), gy: 4 (over z).
Axes of the slice: x: 2, y: 2, z: 4, core: 2. Of those that a mesh axis runs over, the one named last changes fastest.
Arguments:
- potential: float32 [64, 1024, 256], P('gx', 'gy'), may hold values from -6 to 6
- classes: int32 [64, 1024, 256], P('gx', 'gy'), may hold values from 0 to 7
- sigma_table: float32 [8], replicated, may hold values from 0.5 to 5
- row_index: int32 [2], replicated, may hold values from 0 to 63
- col_index: int32 [2], replicated, may hold values from 0 to 1023
- depth_index: int32 [2], replicated, may hold values from 0 to 255
- currents: float32 [2], replicated, may hold values from -60 to 60
Outputs:
- new_potential: float32 [64, 1024, 256], P('gx', 'gy')
The draws below stay inside these ranges and needn't reach their ends.
All inputs are finite; a program needn't handle non-finite values.
Results may differ from the reference program's by a relative error of at most 0.0003.
Values sent between devices are 32-bit elements; how exact they have to be, the bound alone decides.
No kernel may reach another device: no remote copies, remote signals or barrier semaphores. Data moves between devices by JAX's collectives and lax.ppermute only.
A program may use at most 128 MiB of HBM per device.

```python
import math
import jax
import jax.numpy as jnp

NZ = 256
NCLASS = 8
NSRC = 2
FSWEEPS = 2
CSWEEPS = 4
NX = 64
NY = 1024


def set_ends(drawn, key, low, largest):
    longest = drawn.shape.index(max(drawn.shape))
    spots = []
    for shift in (0, 1):
        where = [jax.random.randint(jax.random.fold_in(key, axis), (), 0, length) for axis, length in enumerate(drawn.shape)]
        where[longest] = (where[longest] + shift) % drawn.shape[longest]
        spots.append(tuple(where))
    return drawn.at[spots[0]].set(low).at[spots[1]].set(largest)


def steps_of(key, shape, cuts, smallest, high):
    def one(dim, shards_of):
        heights = jax.random.uniform(jax.random.fold_in(jax.random.fold_in(key, 6), dim), (shards_of,), jnp.float32, smallest / len(cuts), high / len(cuts))
        return jnp.repeat(jnp.exp(heights), shape[dim] // shards_of).reshape((-1,) + (1,) * (len(shape) - dim - 1))

    gain = one(*cuts[0])
    for cut in cuts[1:]:
        gain = gain * one(*cut)
    return gain


def centred(own_key, extent, scale, most, split=(), held_as=jnp.bfloat16):
    entries = jax.random.normal(own_key, extent, jnp.float32) * scale
    if len(split) > 0:
        entries = steps_of(own_key, extent, split, -0.22, 0.18) * entries
    return jnp.clip(entries, min=-most, max=most).astype(held_as)


def setup_inputs(seed: int = 0) -> dict:
    key_of = jax.random.split(jax.random.key(seed), 8)
    potential = centred(key_of[0], (NX, NY, NZ), 1.0, 6.0, ((0, 8), (1, 4)), jnp.float32)
    classes = set_ends(jax.random.randint(key_of[1], (NX, NY, NZ), 0, NCLASS), jax.random.fold_in(key_of[1], 1), 0, NCLASS - 1).astype(jnp.int32)
    sigma_table = jnp.clip(jnp.exp(jax.random.uniform(key_of[2], (NCLASS,), jnp.float32, math.log(0.5), math.log(5.0))), 0.5, 5.0)
    row_index = jax.random.randint(key_of[3], (NSRC,), 0, NX).astype(jnp.int32)
    col_index = jax.random.randint(key_of[4], (NSRC,), 0, NY).astype(jnp.int32)
    depth_index = jax.random.randint(key_of[5], (NSRC,), 0, NZ).astype(jnp.int32)
    currents = jnp.clip(jax.random.uniform(key_of[6], (NSRC,), jnp.float32, -60.0, 60.0), -60.0, 60.0)
    return dict(potential=potential, classes=classes, sigma_table=sigma_table, row_index=row_index, col_index=col_index, depth_index=depth_index, currents=currents)


OMEGA = 0.8


def face_pair(own_sigma, near_sigma):
    pair_sum = own_sigma + near_sigma
    safe_sum = jnp.where(pair_sum > 0, pair_sum, 1.0)
    return jnp.where(near_sigma > 0, 2.0 * own_sigma * near_sigma / safe_sum, 2.0 * own_sigma)


def six_faces(sigma_ext):
    own_sigma = sigma_ext[1:-1, 1:-1]
    depth_padded = jnp.pad(own_sigma, ((0, 0), (0, 0), (1, 1)))
    return (face_pair(own_sigma, sigma_ext[:-2, 1:-1]), face_pair(own_sigma, sigma_ext[2:, 1:-1]),
            face_pair(own_sigma, sigma_ext[1:-1, :-2]), face_pair(own_sigma, sigma_ext[1:-1, 2:]),
            face_pair(own_sigma, depth_padded[:, :, :-2]), face_pair(own_sigma, depth_padded[:, :, 2:]))


def apply_op(padded, face_set):
    middle = padded[1:-1, 1:-1]
    depth_padded = jnp.pad(middle, ((0, 0), (0, 0), (1, 1)))
    diagonal = face_set[0] + face_set[1] + face_set[2] + face_set[3] + face_set[4] + face_set[5]
    beside = face_set[0] * padded[:-2, 1:-1] + face_set[1] * padded[2:, 1:-1]
    beside = beside + face_set[2] * padded[1:-1, :-2] + face_set[3] * padded[1:-1, 2:]
    beside = beside + face_set[4] * depth_padded[:, :, :-2] + face_set[5] * depth_padded[:, :, 2:]
    return diagonal * middle - beside, diagonal


def relax(padded, face_set, source):
    image, diagonal = apply_op(padded, face_set)
    safe_diag = jnp.where(diagonal > 0, diagonal, 1.0)
    return padded[1:-1, 1:-1] + OMEGA * (source - image) / safe_diag


def pad_plane(field):
    return jnp.pad(field, ((1, 1), (1, 1), (0, 0)))


def split_cells(field):
    return field.reshape(field.shape[0] // 2, 2, field.shape[1] // 2, 2, field.shape[2] // 2, 2)


def coarsen(face_set):
    return (split_cells(face_set[0])[:, 0].sum(axis=(2, 4)), split_cells(face_set[1])[:, 1].sum(axis=(2, 4)),
            split_cells(face_set[2])[:, :, :, 0].sum(axis=(1, 4)), split_cells(face_set[3])[:, :, :, 1].sum(axis=(1, 4)),
            split_cells(face_set[4])[..., 0].sum(axis=(1, 3)), split_cells(face_set[5])[..., 1].sum(axis=(1, 3)))


def reference(potential, classes, sigma_table, row_index, col_index, depth_index, currents):
    sigma = sigma_table[classes]
    face_set = six_faces(pad_plane(sigma))
    source = jnp.zeros_like(potential).at[row_index, col_index, depth_index].add(currents)
    field = potential
    for sweep_id in range(FSWEEPS):
        field = relax(pad_plane(field), face_set, source)
    image, diagonal = apply_op(pad_plane(field), face_set)
    resid = source - image
    coarse_resid = split_cells(resid).sum(axis=(1, 3, 5))
    coarse_faces = coarsen(face_set)
    correction = jnp.zeros_like(coarse_resid)
    for sweep_id in range(CSWEEPS):
        correction = relax(pad_plane(correction), coarse_faces, coarse_resid)
    fine_shape = (NX // 2, 2, NY // 2, 2, NZ // 2, 2)
    field = field + jnp.broadcast_to(correction[:, None, :, None, :, None], fine_shape).reshape(NX, NY, NZ)
    for sweep_id in range(FSWEEPS):
        field = relax(pad_plane(field), face_set, source)
    return field
```

```python
import functools

import jax
import jax.numpy as jnp
from jax import lax
from jax.experimental import pallas as pl
from jax.experimental.pallas import tpu as pltpu
from jax.sharding import PartitionSpec as P

OMEGA = 0.8
HALO = 16
PAD = 8
LANES = 128
CHUNK = 32
F32 = jnp.float32
XL, XU, YL, YU, ZL, ZU = range(6)

VM = pl.BlockSpec(memory_space=pltpu.VMEM)
SM = pl.BlockSpec(memory_space=pltpu.SMEM)


class Dims:
    def __init__(self, shape):
        self.rows, self.cols, self.depth = shape
        self.halves = self.depth // LANES
        self.ext = self.cols + 2 * HALO
        self.padded = self.ext + 2 * PAD
        self.crows = self.rows // 2
        self.cext = self.ext // 2


def chunks(total, size, fn):
    def step(i, carry):
        fn(pl.multiple_of(i * size, 8))
        return carry

    lax.fori_loop(0, total // size, step, 0)


def lanes_of(rows):
    return lax.broadcasted_iota(jnp.int32, (rows, LANES), 1)


def below(parts):
    rolled = [pltpu.roll(part, 1, 1) for part in parts]
    first = lanes_of(parts[0].shape[0]) == 0
    return [rolled[0]] + [
        jnp.where(first, rolled[h - 1], rolled[h]) for h in range(1, len(parts))
    ]


def above(parts):
    rolled = [pltpu.roll(part, LANES - 1, 1) for part in parts]
    last = lanes_of(parts[0].shape[0]) == LANES - 1
    return [
        jnp.where(last, rolled[h + 1], rolled[h]) for h in range(len(parts) - 1)
    ] + [rolled[-1]]


def face(total):
    return jnp.where(total > 0, 2.0 / total, 0.0)


def lookup(cells, table):
    bits = [(cells & (1 << b)) != 0 for b in range(3)]
    level = [table[k] for k in range(8)]
    for bit in bits:
        level = [jnp.where(bit, level[k + 1], level[k]) for k in range(0, len(level), 2)]
    return level[0]


def sweep(dims, below_row, row, above_row, weights, out, scale=None, total=None):
    def body(y0):
        here = [row[h, pl.ds(y0 + PAD, CHUNK), :] for h in range(dims.halves)]
        zlow, zhigh = below(here), above(here)
        for h in range(dims.halves):
            span, wide = pl.ds(y0, CHUNK), pl.ds(y0 + PAD, CHUNK)
            acc = weights[XL][h, span, :] * below_row[h, wide, :]
            acc += weights[XU][h, span, :] * above_row[h, wide, :]
            acc += weights[YL][h, span, :] * row[h, pl.ds(y0 + PAD - 1, CHUNK), :]
            acc += weights[YU][h, span, :] * row[h, pl.ds(y0 + PAD + 1, CHUNK), :]
            acc += weights[ZL][h, span, :] * zlow[h]
            acc += weights[ZU][h, span, :] * zhigh[h]
            if scale is None:
                out[h, wide, :] = acc + (1.0 - OMEGA) * here[h]
            else:
                out[h, span, :] = (acc - OMEGA * here[h]) * scale[h, span, :]

    chunks(dims.ext, CHUNK, body)


def sources(dims, meta, cur, count, targets, fix):
    for s in range(count):
        row, col, dep = meta[s], meta[count + s], meta[2 * count + s]
        ext_col = col + HALO

        @pl.when(
            (row >= targets[0]) & (row <= targets[-1]) & (ext_col >= 0) & (ext_col < dims.ext)
        )
        def _():
            for x in targets:

                @pl.when(row == x)
                def _(x=x):
                    for h in range(dims.halves):
                        hit = lanes_of(1) == dep - h * LANES
                        fix(x, ext_col, h, jnp.where(hit, cur[s], 0.0))


def add_swept(field, scale, col, h, amount):
    field[h, pl.ds(col + PAD, 1), :] += amount / scale[h, pl.ds(col, 1), :]


def row_faces(dims, row, row_below_faces, yl_out, zl_out, xl_out):
    def body(y0):
        here = [row[h, pl.ds(y0 + PAD, CHUNK), :] for h in range(dims.halves)]
        zlow = below(here)
        first = lanes_of(CHUNK) == 0
        zlow[0] = jnp.where(first, 0.0, zlow[0])
        for h in range(dims.halves):
            wide = pl.ds(y0 + PAD, CHUNK)
            if xl_out is not None:
                xl_out[h, pl.ds(y0, CHUNK), :] = face(here[h] + row_below_faces[h, wide, :])
            if yl_out is not None:
                yl_out[h, wide, :] = face(here[h] + row[h, pl.ds(y0 + PAD - 1, CHUNK), :])
                zl_out[h, pl.ds(y0, CHUNK), :] = face(here[h] + zlow[h])

    chunks(dims.ext, CHUNK, body)


def row_weights(dims, row, xl, xu, yl, zl, weights, scale):
    def body(y0):
        span, wide = pl.ds(y0, CHUNK), pl.ds(y0 + PAD, CHUNK)
        low = [zl[h, span, :] for h in range(dims.halves)]
        high = above(low)
        lane = lanes_of(CHUNK)
        top = dims.halves - 1
        high[top] = jnp.where(lane == LANES - 1, face(row[top, wide, :]), high[top])
        for h in range(dims.halves):
            parts = [
                xl[h, span, :],
                xu[h, span, :],
                yl[h, wide, :],
                yl[h, pl.ds(y0 + PAD + 1, CHUNK), :],
                low[h],
                high[h],
            ]
            diag = parts[0] + parts[1] + parts[2] + parts[3] + parts[4] + parts[5]
            gain = jnp.where(row[h, wide, :] > 0, OMEGA / diag, 0.0)
            scale[h, span, :] = diag * (1.0 / OMEGA)
            if h == 0:
                parts[ZL] = jnp.where(lane == 0, 0.0, parts[ZL])
            if h == top:
                parts[ZU] = jnp.where(lane == LANES - 1, 0.0, parts[ZU])
            for k in range(6):
                weights[k][h, span, :] = gain * parts[k]

    chunks(dims.ext, CHUNK, body)


def split_dot(field, chosen):
    total = None
    for _ in range(3):
        piece = field.astype(jnp.bfloat16)
        field = field - piece.astype(F32)
        term = jnp.dot(piece, chosen, preferred_element_type=F32)
        total = term if total is None else total + term
    return total


def picker(dims, h, lowest, highest):
    fine = lax.broadcasted_iota(jnp.int32, (LANES, LANES), 0) + h * LANES
    coarse = lax.broadcasted_iota(jnp.int32, (LANES, LANES), 1)
    hit = (fine >= 2 * coarse + lowest) & (fine <= 2 * coarse + highest)
    return jnp.where(hit, 1.0, 0.0).astype(jnp.bfloat16)


def restrict(dims, rows, offset, parities, chosen):
    total = None
    for h in range(dims.halves):
        acc = None
        for row in rows:
            for parity in parities:
                part = row[h, pl.ds(offset + parity, dims.cext, stride=2), :]
                acc = part if acc is None else acc + part
        term = split_dot(acc, chosen[h])
        total = term if total is None else total + term
    return total


def first_kernel(dims, nsrc, meta, cur, table, pot, cls, yod, yev, *refs):
    (wts, scl, one, two, rsd, eres, evol, efx, efy, efz, cfc, ins, send_od, send_ev) = refs[:14]
    res, vol, fx, fy, fz = refs[14:]
    rows, halves, cols = dims.rows, dims.halves, dims.cols
    odd_x, odd_y = meta[3 * nsrc] == 1, meta[3 * nsrc + 1] == 1
    lanes = [slice(h * LANES, (h + 1) * LANES) for h in range(halves)]

    def halo_res(code):
        number = code.astype(jnp.int32)
        return jnp.where(number > 0, lookup(number - 1, table), 0.0)

    def assemble(x, carry):
        for h in range(halves):
            zero = jnp.zeros((PAD, LANES), F32)
            for ref in (res, vol):
                ref[x, h, pl.ds(0, PAD), :] = zero
                ref[x, h, pl.ds(PAD + dims.ext, PAD), :] = zero
            for into, take_ev in ((PAD, True), (PAD + HALO + cols, False)):
                pair = []
                for k in range(2):
                    a, b = yod[k, x, :, lanes[h]], yev[k, x, :, lanes[h]]
                    pair.append(jnp.where(odd_y, b, a) if take_ev else jnp.where(odd_y, a, b))
                vol[x, h, pl.ds(into, HALO), :] = pair[0]
                res[x, h, pl.ds(into, HALO), :] = halo_res(pair[1])

            def own(y0):
                vol[x, h, pl.ds(y0 + PAD + HALO, CHUNK), :] = pot[x, pl.ds(y0, CHUNK), lanes[h]]
                res[x, h, pl.ds(y0 + PAD + HALO, CHUNK), :] = lookup(
                    cls[x, pl.ds(y0, CHUNK), lanes[h]], table
                )

            chunks(cols, CHUNK, own)
        return carry

    lax.fori_loop(0, rows, assemble, 0)

    for x in range(rows):
        for h in range(halves):
            fy[x, h, pl.ds(PAD + dims.ext, PAD), :] = jnp.zeros((PAD, LANES), F32)
        row_faces(
            dims,
            res.at[x],
            res.at[x - 1] if x else None,
            fy.at[x],
            fz.at[x],
            fx.at[x] if x else None,
        )
    for x in range(1, rows - 1):
        row_weights(
            dims,
            res.at[x],
            fx.at[x],
            fx.at[x + 1],
            fy.at[x],
            fz.at[x],
            [wts.at[k, x - 1] for k in range(6)],
            scl.at[x - 1],
        )
    weights = lambda x: [wts.at[k, x - 1] for k in range(6)]

    for x in range(1, rows - 1):
        sweep(dims, vol.at[x - 1], vol.at[x], vol.at[x + 1], weights(x), one.at[x - 1])

    sources(
        dims, meta, cur, nsrc, range(1, rows - 1),
        lambda x, *rest: add_swept(one.at[x - 1], scl.at[x - 1], *rest),
    )

    def fill(send, high):
        edge = jnp.where(high, rows - 2, 0)
        inner = jnp.where(high, rows - 2, 1)
        for h in range(halves):
            send[pl.ds(h * dims.ext, dims.ext), :] = one[inner - 1, h, pl.ds(PAD, dims.ext), :]
        base = halves * dims.ext
        for k in range(4):
            ref = vol if k < 2 else res
            for h in range(halves):
                at = base + (k * halves + h) * 2 * HALO
                send[pl.ds(at, HALO), :] = ref[edge + k % 2, h, pl.ds(PAD, HALO), :]
                send[pl.ds(at + HALO, HALO), :] = ref[
                    edge + k % 2, h, pl.ds(PAD + HALO + cols, HALO), :
                ]

    fill(send_od, odd_x)
    fill(send_ev, jnp.logical_not(odd_x))

    for x in range(2, rows - 2):
        sweep(dims, one.at[x - 2], one.at[x - 1], one.at[x], weights(x), two.at[x - 2])

    sources(
        dims, meta, cur, nsrc, range(2, rows - 2),
        lambda x, *rest: add_swept(two.at[x - 2], scl.at[x - 1], *rest),
    )

    for x in range(3, rows - 3):
        sweep(
            dims, two.at[x - 3], two.at[x - 2], two.at[x - 1], weights(x), rsd.at[x - 3],
            scl.at[x - 1],
        )

    def fix_rsd(row, col, h, amount):
        rsd[row - 3, h, pl.ds(col, 1), :] += amount

    sources(dims, meta, cur, nsrc, range(3, rows - 3), fix_rsd)

    def keep(y0):
        span, wide = pl.ds(y0, CHUNK), pl.ds(y0 + PAD, CHUNK)
        for h in range(halves):
            for k, x in enumerate((0, rows - 1)):
                eres[k, h, wide, :] = res[x, h, wide, :]
                efy[k, h, wide, :] = fy[x, h, wide, :]
                efz[k, h, span, :] = fz[x, h, span, :]
            for k, x in enumerate((0, 1, rows - 2, rows - 1)):
                evol[k, h, wide, :] = vol[x, h, wide, :]
            for k, x in enumerate((1, rows - 1)):
                efx[k, h, span, :] = fx[x, h, span, :]

    chunks(dims.ext, CHUNK, keep)
    for h in range(halves):
        zeros = jnp.zeros((PAD, LANES), F32)
        for ref, count in ((eres, 2), (efy, 2), (evol, 4)):
            for k in range(count):
                ref[k, h, pl.ds(0, PAD), :] = zeros
                ref[k, h, pl.ds(PAD + dims.ext, PAD), :] = zeros

    both = [picker(dims, h, 0, 1) for h in range(halves)]
    even = [picker(dims, h, 0, 0) for h in range(halves)]
    n = dims.crows
    for c in range(n):
        pair = lambda ref: [ref.at[2 * c], ref.at[2 * c + 1]]
        if c:
            cfc[c] = restrict(dims, [fx.at[2 * c]], 0, (0, 1), both)
        cfc[n + 1 + c] = restrict(dims, pair(fy), PAD, (0,), both)
        cfc[2 * n + 1 + c] = restrict(dims, pair(fz), 0, (0, 1), even)
        top = None
        for row in pair(res):
            for parity in (0, 1):
                part = face(row[halves - 1, pl.ds(PAD + parity, dims.cext, stride=2), :])
                top = part if top is None else top + part
        cfc[3 * n + 1 + c] = top
        ins[c] = res[2 * c, 0, pl.ds(PAD, dims.cext, stride=2), :]


def neighbours(rows):
    ext = rows.shape[0]
    return (
        pltpu.roll(rows, 1, 0),
        pltpu.roll(rows, ext - 1, 0),
        pltpu.roll(rows, 1, 1),
        pltpu.roll(rows, LANES - 1, 1),
    )


def coarse_side(field, base, weights):
    ylow, yhigh, zlow, zhigh = neighbours(field)
    return (
        (1.0 - OMEGA) * field
        + base
        + weights[YL] * ylow
        + weights[YU] * yhigh
        + weights[ZL] * zlow
        + weights[ZU] * zhigh
    )


def second_kernel(dims, nsrc, meta, cur, table, xod, xev, sod, sev, wts, scl, one, two, rsd, res,
                  vol, fx, fy, fz, cfc, ins, hwts, hscl, htwo, gco, base, c_od, c_ev, v_od, v_ev,
                  hres, hvol, hfx, hfy, hfz, edge, redge):
    rows, halves, cols = dims.rows, dims.halves, dims.cols
    odd_x = meta[3 * nsrc] == 1
    lanes = [slice(h * LANES, (h + 1) * LANES) for h in range(halves)]
    last = rows - 1

    def halo_res(code):
        number = code.astype(jnp.int32)
        return jnp.where(number > 0, lookup(number - 1, table), 0.0)

    for side in range(2):
        choose = lambda a, b: jnp.where(odd_x, b, a) if side == 0 else jnp.where(odd_x, a, b)
        for k in range(2):
            at = 2 * side + k
            for h in range(halves):
                zero = jnp.zeros((PAD, LANES), F32)
                for ref in (hres, hvol):
                    ref[at, h, pl.ds(0, PAD), :] = zero
                    ref[at, h, pl.ds(PAD + dims.ext, PAD), :] = zero
                for ref, kind in ((hvol, k), (hres, 2 + k)):
                    strip = halves * dims.ext + (kind * halves + h) * 2 * HALO
                    low = pl.ds(strip, HALO)
                    high = pl.ds(strip + HALO, HALO)
                    ref[at, h, pl.ds(PAD, HALO), :] = choose(sod[low, :], sev[low, :])
                    ref[at, h, pl.ds(PAD + HALO + cols, HALO), :] = choose(
                        sod[high, :], sev[high, :]
                    )

                def own(y0):
                    span = pl.ds(y0, CHUNK)
                    wide = pl.ds(y0 + PAD + HALO, CHUNK)
                    hvol[at, h, wide, :] = choose(xod[k, span, lanes[h]], xev[k, span, lanes[h]])
                    hres[at, h, wide, :] = halo_res(
                        choose(xod[2 + k, span, lanes[h]], xev[2 + k, span, lanes[h]])
                    )

                chunks(cols, CHUNK, own)
        for h in range(halves):

            def swept(y0):
                span = pl.ds(h * dims.ext + y0, CHUNK)
                edge[5 * side, h, pl.ds(y0 + PAD, CHUNK), :] = choose(sod[span, :], sev[span, :])

            chunks(dims.ext, CHUNK, swept)

    row_faces(dims, hres.at[1], hres.at[0], hfy.at[0], hfz.at[0], hfx.at[0])
    row_faces(dims, res.at[0], hres.at[1], None, None, hfx.at[1])
    row_faces(dims, hres.at[2], res.at[1], hfy.at[1], hfz.at[1], hfx.at[2])
    row_faces(dims, hres.at[3], hres.at[2], None, None, hfx.at[3])
    for side in range(2):
        for h in range(halves):
            hfy[side, h, pl.ds(PAD + dims.ext, PAD), :] = jnp.zeros((PAD, LANES), F32)

    outer = lambda x: x + 1 if x <= 0 else x - last + 2
    inner = lambda x: 1 <= x <= last - 1
    weights = lambda x: [
        wts.at[k, x - 1] if inner(x) else hwts.at[k, outer(x)] for k in range(6)
    ]
    scale = lambda x: scl.at[x - 1] if inner(x) else hscl.at[outer(x)]
    for x, row, xl, xu, yl, zl in (
        (-1, hres.at[1], hfx.at[0], hfx.at[1], hfy.at[0], hfz.at[0]),
        (0, res.at[0], hfx.at[1], fx.at[0], fy.at[0], fz.at[0]),
        (last, res.at[1], fx.at[1], hfx.at[2], fy.at[1], fz.at[1]),
        (rows, hres.at[2], hfx.at[2], hfx.at[3], hfy.at[1], hfz.at[1]),
    ):
        row_weights(dims, row, xl, xu, yl, zl, weights(x), scale(x))

    def start(x):
        if x < 0:
            return hvol.at[x + 2]
        if x >= rows:
            return hvol.at[x - rows + 2]
        return vol.at[x if x <= 1 else x - last + 3]

    def swept(x):
        if x <= 0:
            return edge.at[x + 2]
        return one.at[x - 1] if x < last else edge.at[x - last + 3]

    for x in (-1, 0, last, rows):
        sweep(dims, start(x - 1), start(x), start(x + 1), weights(x), swept(x))

    sources(
        dims, meta, cur, nsrc, (-1, 0, last, rows),
        lambda x, *rest: add_swept(swept(x), scale(x), *rest),
    )

    def twice(x):
        if x <= 1:
            return htwo.at[x + 1]
        return two.at[x - 2] if x < last - 1 else htwo.at[x - last + 4]

    for x in (-1, 0, 1, last - 1, last, rows):
        sweep(dims, swept(x - 1), swept(x), swept(x + 1), weights(x), twice(x))
    sources(
        dims, meta, cur, nsrc, (-1, 0, 1, last - 1, last, rows),
        lambda x, *rest: add_swept(twice(x), scale(x), *rest),
    )

    def resid_row(x):
        if x <= 2:
            return redge.at[x]
        return rsd.at[x - 3] if x < last - 2 else redge.at[x - last + 5]

    for x in (0, 1, 2, last - 2, last - 1, last):
        sweep(
            dims, twice(x - 1), twice(x), twice(x + 1), weights(x), resid_row(x), scale(x)
        )

    def fix_rsd(x, col, h, amount):
        resid_row(x)[h, pl.ds(col, 1), :] += amount

    sources(dims, meta, cur, nsrc, (0, 1, 2, last - 2, last - 1, last), fix_rsd)

    both = [picker(dims, h, 0, 1) for h in range(halves)]
    n = dims.crows
    lane = lanes_of(dims.cext)
    bottom = restrict(dims, [hfx.at[1]], 0, (0, 1), both)
    topmost = restrict(dims, [hfx.at[2]], 0, (0, 1), both)

    e1, gc = [], []
    for c in range(n):
        xl = bottom if c == 0 else cfc[c]
        xu = topmost if c == n - 1 else cfc[c + 1]
        yl, zl = cfc[n + 1 + c], cfc[2 * n + 1 + c]
        yu = pltpu.roll(yl, dims.cext - 1, 0)
        zu = jnp.where(lane == LANES - 1, cfc[3 * n + 1 + c], pltpu.roll(zl, LANES - 1, 1))
        diag = xl + xu + yl + yu + zl + zu
        inside = ins[c] > 0
        gain = jnp.where(inside, OMEGA / diag, 0.0)
        zl = jnp.where(lane == 0, 0.0, zl)
        zu = jnp.where(lane == LANES - 1, 0.0, zu)
        gc.append([gain * part for part in (xl, xu, yl, yu, zl, zu)])
        for k in range(6):
            gco[k, c] = gc[c][k]
        total = restrict(dims, [resid_row(2 * c), resid_row(2 * c + 1)], 0, (0, 1), both)
        e1.append(gain * total)
        base[c] = e1[c]

    low = (e1[0], coarse_side(e1[0], e1[0], gc[0]) + gc[0][XU] * e1[1], gc[0][XL])
    high = (
        e1[n - 1],
        coarse_side(e1[n - 1], e1[n - 1], gc[n - 1]) + gc[n - 1][XL] * e1[n - 2],
        gc[n - 1][XU],
    )
    for k in range(3):
        c_od[k] = jnp.where(odd_x, high[k], low[k])
        c_ev[k] = jnp.where(odd_x, low[k], high[k])
    pick_od = jnp.where(odd_x, 3, 2)
    pick_ev = jnp.where(odd_x, 2, 3)
    for h in range(halves):

        def out(y0):
            wide = pl.ds(y0 + PAD, CHUNK)
            v_od[h, pl.ds(y0, CHUNK), :] = htwo[pick_od, h, wide, :]
            v_ev[h, pl.ds(y0, CHUNK), :] = htwo[pick_ev, h, wide, :]

        chunks(dims.ext, CHUNK, out)


def third_kernel(dims, nsrc, meta, gco, base, rod, rev, e3, c_od, c_ev):
    n = dims.crows
    odd_x = meta[3 * nsrc] == 1
    low = [jnp.where(odd_x, rev[k], rod[k]) for k in range(3)]
    high = [jnp.where(odd_x, rod[k], rev[k]) for k in range(3)]
    gc = lambda c: [gco[k, c] for k in range(6)]

    def coarse_sweep(field, under, over):
        out = []
        for c in range(n):
            w = gc(c)
            new = coarse_side(field[c], base[c], w)
            new += w[XL] * (field[c - 1] if c else under)
            new += w[XU] * (field[c + 1] if c < n - 1 else over)
            out.append(new)
        return out

    e1 = [base[c] for c in range(n)]
    e2 = coarse_sweep(e1, low[0], high[0])
    under = low[1] + low[2] * e1[0]
    over = high[1] + high[2] * e1[n - 1]
    out = coarse_sweep(e2, under, over)
    for c in range(n):
        e3[c] = out[c]
    w = gc(0)
    first = (out[0], coarse_side(out[0], base[0], w) + w[XU] * out[1])
    w = gc(n - 1)
    final = (out[n - 1], coarse_side(out[n - 1], base[n - 1], w) + w[XL] * out[n - 2])
    for k in range(2):
        c_od[k] = jnp.where(odd_x, final[k], first[k])
        c_ev[k] = jnp.where(odd_x, first[k], final[k])


def fourth_kernel(dims, nsrc, meta, cur, gco, base, e3, rod, rev, tod, tev, vod, vev, wts, scl, two,
                  hwts, hscl, htwo, out, raised, zero, three, done, sems):
    rows, halves, cols = dims.rows, dims.halves, dims.cols
    n = dims.crows
    odd_x = meta[3 * nsrc] == 1
    below_of = lambda od, ev: jnp.where(odd_x, ev, od)
    above_of = lambda od, ev: jnp.where(odd_x, od, ev)
    field = [e3[c] for c in range(n)]
    under = below_of(tod[1], tev[1]) + below_of(rod[2], rev[2]) * field[0]
    over = above_of(tod[1], tev[1]) + above_of(rod[2], rev[2]) * field[n - 1]
    e4 = [under]
    for c in range(n):
        w = [gco[k, c] for k in range(6)]
        new = coarse_side(field[c], base[c], w)
        new += w[XL] * (field[c - 1] if c else below_of(tod[0], tev[0]))
        new += w[XU] * (field[c + 1] if c < n - 1 else above_of(tod[0], tev[0]))
        e4.append(new)
    e4.append(over)
    spread = []
    for h in range(halves):
        fine = lax.broadcasted_iota(jnp.int32, (LANES, LANES), 1) + h * LANES
        coarse = lax.broadcasted_iota(jnp.int32, (LANES, LANES), 0)
        hit = (fine >= 2 * coarse) & (fine <= 2 * coarse + 1)
        spread.append(jnp.where(hit, 1.0, 0.0).astype(jnp.bfloat16))
    for c in range(n + 2):
        for h in range(halves):
            lifted = split_dot(e4[c], spread[h])
            raised[c, h, pl.ds(0, dims.cext, stride=2), :] = lifted
            raised[c, h, pl.ds(1, dims.cext, stride=2), :] = lifted

    last = rows - 1

    def twice(x):
        if x <= 1:
            return htwo.at[x + 1]
        return two.at[x - 2] if x < last - 1 else htwo.at[x - last + 4]

    outer = lambda x: x + 1 if x <= 0 else x - last + 2
    inner = lambda x: 1 <= x <= last - 1
    weights = lambda x: [
        wts.at[k, x - 1] if inner(x) else hwts.at[k, outer(x)] for k in range(6)
    ]
    scale = lambda x: scl.at[x - 1] if inner(x) else hscl.at[outer(x)]
    for x in range(-2, rows + 2):
        for h in range(halves):

            def add(y0):
                span, wide = pl.ds(y0, CHUNK), pl.ds(y0 + PAD, CHUNK)
                if x == -2:
                    value = below_of(vod[h, span, :], vev[h, span, :])
                elif x == rows + 1:
                    value = above_of(vod[h, span, :], vev[h, span, :])
                else:
                    value = twice(x)[h, wide, :]
                zero[x + 2, h, wide, :] = value + raised[(x + 2) // 2, h, span, :]

            chunks(dims.ext, CHUNK, add)

    for x in range(-1, rows + 1):
        sweep(dims, zero.at[x + 1], zero.at[x + 2], zero.at[x + 3], weights(x), three.at[x + 1])

    sources(
        dims, meta, cur, nsrc, range(-1, rows + 1),
        lambda x, *rest: add_swept(three.at[x + 1], scale(x), *rest),
    )

    copies = []
    for x in range(rows):
        below_row, row, above_row = three.at[x], three.at[x + 1], three.at[x + 2]
        w = weights(x)

        def body(y0):
            at = y0 + PAD + HALO
            here = [row[h, pl.ds(at, CHUNK), :] for h in range(halves)]
            zlow, zhigh = below(here), above(here)
            for h in range(halves):
                span = pl.ds(y0 + HALO, CHUNK)
                acc = w[XL][h, span, :] * below_row[h, pl.ds(at, CHUNK), :]
                acc += w[XU][h, span, :] * above_row[h, pl.ds(at, CHUNK), :]
                acc += w[YL][h, span, :] * row[h, pl.ds(at - 1, CHUNK), :]
                acc += w[YU][h, span, :] * row[h, pl.ds(at + 1, CHUNK), :]
                acc += w[ZL][h, span, :] * zlow[h]
                acc += w[ZU][h, span, :] * zhigh[h]
                done[x, pl.ds(y0, CHUNK), h * LANES : (h + 1) * LANES] = (
                    acc + (1.0 - OMEGA) * here[h]
                )

        chunks(cols, CHUNK, body)

        for s in range(nsrc):
            r, col, dep = meta[s], meta[nsrc + s], meta[2 * nsrc + s]

            @pl.when((r == x) & (col >= 0) & (col < cols))
            def _():
                for h in range(halves):
                    block = pl.multiple_of(col // 8 * 8, 8)
                    place = lax.broadcasted_iota(jnp.int32, (8, LANES), 0) + block
                    hit = (lanes_of(8) == dep - h * LANES) & (place == col)
                    amount = jnp.where(hit, cur[s], 0.0)
                    done[x, pl.ds(block, 8), h * LANES : (h + 1) * LANES] += (
                        amount / scale(x)[h, pl.ds(block + HALO, 8), :]
                    )

        copy = pltpu.make_async_copy(done.at[x], out.at[x], sems.at[x])
        copy.start()
        copies.append(copy)
    for copy in copies:
        copy.wait()


def call(kernel, outs, ins, specs, scratch=(), aliases=None, out_specs=None, limit=24, cost=1):
    return pl.pallas_call(
        kernel,
        out_shape=[jax.ShapeDtypeStruct(shape, F32) for shape in outs],
        in_specs=specs,
        out_specs=out_specs if out_specs is not None else [VM] * len(outs),
        scratch_shapes=list(scratch),
        input_output_aliases=aliases or {},
        compiler_params=pltpu.CompilerParams(vmem_limit_bytes=limit * 2**20),
        cost_estimate=pl.CostEstimate(flops=cost, bytes_accessed=cost, transcendentals=0),
    )(*ins)


def swaps(count):
    pairs = []
    for first in (1, 0):
        found = []
        for low in range(first, count - 1, 2):
            found += [(low, low + 1), (low + 1, low)]
        pairs.append(found)
    return pairs


def swap(od, ev, axis):
    odd_pairs, even_pairs = swaps(lax.axis_size(axis))
    return lax.ppermute(od, axis, odd_pairs), lax.ppermute(ev, axis, even_pairs)


def per_device(potential, classes, sigma_table, row_index, col_index, depth_index, currents):
    dims = Dims(potential.shape)
    rows, cols, depth = potential.shape
    halves, ext, padded, n, cext = dims.halves, dims.ext, dims.padded, dims.crows, dims.cext
    nsrc = row_index.shape[0]
    gx, gy = lax.axis_index("gx"), lax.axis_index("gy")
    odd_x, odd_y = gx % 2, gy % 2
    meta = jnp.concatenate(
        [
            row_index - gx * rows,
            col_index - gy * cols,
            depth_index,
            jnp.stack([odd_x, odd_y]),
        ]
    ).astype(jnp.int32)
    table = 1.0 / sigma_table

    def edges(dim, width, high):
        start = jnp.where(high, potential.shape[dim] - width, 0)
        return [
            lax.dynamic_slice_in_dim(potential, start, width, dim),
            lax.dynamic_slice_in_dim(classes, start, width, dim).astype(F32) + 1.0,
        ]

    xod, xev = swap(
        jnp.concatenate(edges(0, 2, odd_x == 1)), jnp.concatenate(edges(0, 2, odd_x == 0)), "gx"
    )
    yod, yev = swap(
        jnp.stack(edges(1, HALO, odd_y == 1)), jnp.stack(edges(1, HALO, odd_y == 0)), "gy"
    )

    bind = lambda kernel: functools.partial(kernel, dims, nsrc)
    wide = lambda k: (k, halves, padded, LANES)
    flat = lambda k: (k, halves, ext, LANES)
    send = (halves * ext + 4 * halves * 2 * HALO, LANES)
    coarse = lambda *k: (*k, cext, LANES)
    (wts, scl, one, two, rsd, res, vol, fx, fy, fz, cfc, ins, sod, sev) = call(
        bind(first_kernel),
        [
            (6, *flat(rows - 2)), flat(rows - 2), wide(rows - 2), wide(rows - 4), flat(rows - 6),
            wide(2), wide(4), flat(2), wide(2), flat(2), coarse(4 * n + 1), coarse(n), send, send,
        ],
        [meta, currents, table, potential, classes, yod, yev],
        [SM, SM, SM, VM, VM, VM, VM],
        scratch=[pltpu.VMEM(shape, F32) for shape in (
            wide(rows), wide(rows), flat(rows), wide(rows), flat(rows))],
        limit=16,
    )
    sod, sev = swap(sod, sev, "gx")
    (hwts, hscl, htwo, gco, base, c_od, c_ev, v_od, v_ev) = call(
        bind(second_kernel),
        [
            (6, *flat(4)), flat(4), wide(6), coarse(6, n), coarse(n),
            coarse(3), coarse(3), flat(1)[1:], flat(1)[1:],
        ],
        [meta, currents, table, xod, xev, sod, sev, wts, scl, one, two, rsd, res, vol, fx, fy, fz,
         cfc, ins],
        [SM] * 3 + [VM] * 16,
        scratch=[pltpu.VMEM(shape, F32) for shape in (
            wide(4), wide(4), flat(4), wide(2), flat(2), wide(6), flat(6))],
        limit=16,
    )
    rod, rev = swap(c_od, c_ev, "gx")
    vod, vev = swap(v_od, v_ev, "gx")
    (e3, t_od, t_ev) = call(
        bind(third_kernel),
        [coarse(n), coarse(2), coarse(2)],
        [meta, gco, base, rod, rev],
        [SM] + [VM] * 4,
        limit=8,
    )
    tod, tev = swap(t_od, t_ev, "gx")
    (out,) = call(
        bind(fourth_kernel),
        [(rows, cols, depth)],
        [meta, currents, gco, base, e3, rod, rev, tod, tev, vod, vev, wts, scl, two, hwts, hscl,
         htwo],
        [SM] * 2 + [VM] * 15,
        scratch=[pltpu.VMEM(shape, F32) for shape in (
            flat(n + 2), wide(rows + 4), wide(rows + 2), (rows, cols, depth))]
        + [pltpu.SemaphoreType.DMA((rows,))],
        out_specs=[pl.BlockSpec(memory_space=pl.ANY)],
        limit=24,
    )
    return out


def solution(mesh):
    tiled = P("gx", "gy", None)
    return jax.shard_map(
        per_device,
        mesh=mesh,
        in_specs=(tiled, tiled, P(), P(), P(), P(), P()),
        out_specs=tiled,
        check_vma=False,
    )
```

```python
import functools

import jax
import jax.numpy as jnp
from jax import lax
from jax.experimental import pallas as pl
from jax.experimental.pallas import tpu as pltpu
from jax.sharding import PartitionSpec as P

OMEGA = 0.8
HALO = 16
PAD = 8
LANES = 128
F32 = jnp.float32
XL, XU, YL, YU, ZL, ZU = range(6)

VM = pl.BlockSpec(memory_space=pltpu.VMEM)
SM = pl.BlockSpec(memory_space=pltpu.SMEM)


class Dims:
    def __init__(self, shape):
        self.rows, self.cols, self.depth = shape
        self.halves = self.depth // LANES
        self.ext = self.cols + 2 * HALO
        self.padded = self.ext + 2 * PAD
        self.crows = self.rows // 2
        self.cext = self.ext // 2
        self.whole = [(0, self.ext)]
        side = HALO + PAD
        self.inside = [(side, self.ext - 2 * side)]
        self.strips = [(0, side), (self.ext - side, side)]


def lanes_of(rows):
    return lax.broadcasted_iota(jnp.int32, (rows, LANES), 1)


def below(parts):
    rolled = [pltpu.roll(part, 1, 1) for part in parts]
    first = lanes_of(parts[0].shape[0]) == 0
    return [rolled[0]] + [
        jnp.where(first, rolled[h - 1], rolled[h]) for h in range(1, len(parts))
    ]


def above(parts):
    rolled = [pltpu.roll(part, LANES - 1, 1) for part in parts]
    last = lanes_of(parts[0].shape[0]) == LANES - 1
    return [
        jnp.where(last, rolled[h + 1], rolled[h]) for h in range(len(parts) - 1)
    ] + [rolled[-1]]


def face(total):
    return jnp.where(total > 0, 2.0 / total, 0.0)


def lookup(cells, table):
    bits = [(cells & (1 << b)) != 0 for b in range(3)]
    level = [table[k] for k in range(8)]
    for bit in bits:
        level = [jnp.where(bit, level[k + 1], level[k]) for k in range(0, len(level), 2)]
    return level[0]


def sweep(dims, below_row, row, above_row, weights, out, scale=None, regions=None):
    for y0, size in regions or dims.whole:
        span, wide = pl.ds(y0, size), pl.ds(y0 + PAD, size)
        here = [row[h, wide, :] for h in range(dims.halves)]
        zlow, zhigh = below(here), above(here)
        for h in range(dims.halves):
            acc = weights[XL][h, span, :] * below_row[h, wide, :]
            acc += weights[XU][h, span, :] * above_row[h, wide, :]
            acc += weights[YL][h, span, :] * row[h, pl.ds(y0 + PAD - 1, size), :]
            acc += weights[YU][h, span, :] * row[h, pl.ds(y0 + PAD + 1, size), :]
            acc += weights[ZL][h, span, :] * zlow[h]
            acc += weights[ZU][h, span, :] * zhigh[h]
            if scale is None:
                out[h, wide, :] = acc + (1.0 - OMEGA) * here[h]
            else:
                out[h, span, :] = (acc - OMEGA * here[h]) * scale[h, span, :]


def sources(dims, meta, cur, count, targets, fix, regions=None):
    for s in range(count):
        row, col, dep = meta[s], meta[count + s], meta[2 * count + s]
        ext_col = col + HALO

        held = None
        for y0, size in regions or dims.whole:
            hit = (ext_col >= y0) & (ext_col < y0 + size)
            held = hit if held is None else held | hit

        @pl.when((row >= targets[0]) & (row <= targets[-1]) & held)
        def _():
            for x in targets:

                @pl.when(row == x)
                def _(x=x):
                    for h in range(dims.halves):
                        hit = lanes_of(1) == dep - h * LANES
                        fix(x, ext_col, h, jnp.where(hit, cur[s], 0.0))


def add_swept(field, scale, col, h, amount):
    field[h, pl.ds(col + PAD, 1), :] += amount / scale[h, pl.ds(col, 1), :]


def row_faces(dims, row, row_below, yl_out, zl_out, xl_out, regions=None):
    for y0, size in regions or dims.whole:
        span, wide = pl.ds(y0, size), pl.ds(y0 + PAD, size)
        here = [row[h, wide, :] for h in range(dims.halves)]
        zlow = below(here)
        zlow[0] = jnp.where(lanes_of(size) == 0, 0.0, zlow[0])
        for h in range(dims.halves):
            if xl_out is not None:
                xl_out[h, span, :] = face(here[h] + row_below[h, wide, :])
            if yl_out is not None:
                yl_out[h, wide, :] = face(here[h] + row[h, pl.ds(y0 + PAD - 1, size), :])
                zl_out[h, span, :] = face(here[h] + zlow[h])


def row_weights(dims, row, xl, xu, yl, zl, weights, scale, regions=None):
    for y0, size in regions or dims.whole:
        span, wide = pl.ds(y0, size), pl.ds(y0 + PAD, size)
        low = [zl[h, span, :] for h in range(dims.halves)]
        high = above(low)
        lane = lanes_of(size)
        top = dims.halves - 1
        high[top] = jnp.where(lane == LANES - 1, face(row[top, wide, :]), high[top])
        for h in range(dims.halves):
            parts = [
                xl[h, span, :],
                xu[h, span, :],
                yl[h, wide, :],
                yl[h, pl.ds(y0 + PAD + 1, size), :],
                low[h],
                high[h],
            ]
            diag = parts[0] + parts[1] + parts[2] + parts[3] + parts[4] + parts[5]
            gain = jnp.where(row[h, wide, :] > 0, OMEGA / diag, 0.0)
            scale[h, span, :] = diag * (1.0 / OMEGA)
            if h == 0:
                parts[ZL] = jnp.where(lane == 0, 0.0, parts[ZL])
            if h == top:
                parts[ZU] = jnp.where(lane == LANES - 1, 0.0, parts[ZU])
            for k in range(6):
                weights[k][h, span, :] = gain * parts[k]


def split_dot(field, chosen):
    total = None
    for _ in range(3):
        piece = field.astype(jnp.bfloat16)
        field = field - piece.astype(F32)
        term = jnp.dot(piece, chosen, preferred_element_type=F32)
        total = term if total is None else total + term
    return total


def picker(dims, h, lowest, highest):
    fine = lax.broadcasted_iota(jnp.int32, (LANES, LANES), 0) + h * LANES
    coarse = lax.broadcasted_iota(jnp.int32, (LANES, LANES), 1)
    hit = (fine >= 2 * coarse + lowest) & (fine <= 2 * coarse + highest)
    return jnp.where(hit, 1.0, 0.0).astype(jnp.bfloat16)


def restrict(dims, rows, offset, parities, chosen):
    total = None
    for h in range(dims.halves):
        acc = None
        for row in rows:
            for parity in parities:
                part = row[h, pl.ds(offset + parity, dims.cext, stride=2), :]
                acc = part if acc is None else acc + part
        term = split_dot(acc, chosen[h])
        total = term if total is None else total + term
    return total


def fetch_edges(parity, dim, width, pot, cls, buffers, kept, sems):
    copies = []
    for k, (pot_out, _) in enumerate(buffers):
        high = parity == (1 - k)
        start = jnp.where(high, pot.shape[dim] - width, 0)
        at = pl.ds(start, width) if dim == 0 else (slice(None), pl.ds(pl.multiple_of(start, 8), width))
        pair = [
            pltpu.make_async_copy(cls.at[at], kept.at[k], sems.at[k, 0]),
            pltpu.make_async_copy(pot.at[at], pot_out, sems.at[k, 1]),
        ]
        for copy in pair:
            copy.start()
        copies.append(pair)
    for k, (_, cls_out) in enumerate(buffers):
        copies[k][0].wait()
        cls_out[...] = kept[k].astype(F32) + 1.0
    for pair in copies:
        pair[1].wait()


def x_edge_kernel(pot, cls, od, ev, kept, sems):
    buffers = [(buf.at[pl.ds(0, 2)], buf.at[pl.ds(2, 2)]) for buf in (od, ev)]
    fetch_edges(lax.axis_index("gx") % 2, 0, 2, pot, cls, buffers, kept, sems)


def y_edge_kernel(pot, cls, od, ev, kept, sems):
    buffers = [(buf.at[0], buf.at[1]) for buf in (od, ev)]
    fetch_edges(lax.axis_index("gy") % 2, 1, HALO, pot, cls, buffers, kept, sems)


def tile_rows(dims, refs):
    rows = dims.rows
    ends, pairs = [0, rows - 1], [0, 1, rows - 2, rows - 1]
    edges = [pairs, pairs, [1, rows - 1], ends, ends]

    def getter(edge, middle, named, first):
        others = [x for x in range(first, rows) if x not in named]
        return lambda x: edge.at[named.index(x)] if x in named else middle.at[others.index(x)]

    found = [getter(refs[k], refs[5 + k], edges[k], int(k == 2)) for k in range(5)]
    return found + list(refs[10:13])


def own_rows(dims, nsrc, meta, cur, res, vol, fx, fy, fz, wts, scl, one, regions, face_regions):
    rows = dims.rows
    for x in range(rows):
        row_faces(
            dims,
            res(x),
            res(x - 1) if x else None,
            fy(x),
            fz(x),
            fx(x) if x else None,
            face_regions,
        )
    weights = lambda x: [wts.at[k, x - 1] for k in range(6)]
    for x in range(1, rows - 1):
        row_weights(
            dims, res(x), fx(x), fx(x + 1), fy(x), fz(x), weights(x),
            scl.at[x - 1], regions,
        )
    for x in range(1, rows - 1):
        sweep(
            dims, vol(x - 1), vol(x), vol(x + 1), weights(x), one.at[x - 1],
            regions=regions,
        )
    sources(
        dims, meta, cur, nsrc, range(1, rows - 1),
        lambda x, *rest: add_swept(one.at[x - 1], scl.at[x - 1], *rest),
        regions,
    )


def tile_kernel(dims, nsrc, meta, cur, table, pot, cls, *refs):
    res, vol, fx, fy, fz, wts, scl, one = tile_rows(dims, refs)
    margin = PAD + HALO
    for x in range(dims.rows):
        for h in range(dims.halves):
            lanes = slice(h * LANES, (h + 1) * LANES)
            zero = jnp.zeros((margin, LANES), F32)
            for ref in (res, vol):
                ref(x)[h, pl.ds(0, margin), :] = zero
                ref(x)[h, pl.ds(margin + dims.cols, margin), :] = zero
            vol(x)[h, pl.ds(margin, dims.cols), :] = pot[x, :, lanes]
            res(x)[h, pl.ds(margin, dims.cols), :] = lookup(cls[x, :, lanes], table)
    own_rows(dims, nsrc, meta, cur, res, vol, fx, fy, fz, wts, scl, one, dims.inside,
             [(HALO, dims.cols)])


def strip_kernel(dims, nsrc, meta, cur, table, yod, yev, *refs):
    count = len(dims.tile)
    res_edge, vol_edge = refs[count], refs[count + 1]
    res, vol, fx, fy, fz, wts, scl, one = tile_rows(dims, refs[count : 2 * count])
    send_od, send_ev = refs[2 * count :]
    rows, halves, cols = dims.rows, dims.halves, dims.cols
    odd_x, odd_y = meta[3 * nsrc] == 1, meta[3 * nsrc + 1] == 1
    for x in range(rows):
        for h in range(halves):
            lanes = slice(h * LANES, (h + 1) * LANES)
            for into, take_ev in ((PAD, True), (PAD + HALO + cols, False)):
                pair = []
                for k in range(2):
                    a, b = yod[k, x, :, lanes], yev[k, x, :, lanes]
                    pair.append(jnp.where(odd_y, b, a) if take_ev else jnp.where(odd_y, a, b))
                vol(x)[h, pl.ds(into, HALO), :] = pair[0]
                number = pair[1].astype(jnp.int32)
                res(x)[h, pl.ds(into, HALO), :] = jnp.where(
                    number > 0, lookup(number - 1, table), 0.0
                )
            fy(x)[h, pl.ds(PAD + dims.ext, PAD), :] = jnp.zeros((PAD, LANES), F32)
    own_rows(dims, nsrc, meta, cur, res, vol, fx, fy, fz, wts, scl, one, dims.strips, dims.strips)

    def fill(send, high):
        edge = jnp.where(high, 2, 0)
        inner = jnp.where(high, rows - 2, 1)
        for h in range(halves):
            send[pl.ds(h * dims.ext, dims.ext), :] = one[inner - 1, h, pl.ds(PAD, dims.ext), :]
        base = halves * dims.ext
        for k in range(4):
            ref = vol_edge if k < 2 else res_edge
            for h in range(halves):
                at = base + (k * halves + h) * 2 * HALO
                send[pl.ds(at, HALO), :] = ref[edge + k % 2, h, pl.ds(PAD, HALO), :]
                send[pl.ds(at + HALO, HALO), :] = ref[
                    edge + k % 2, h, pl.ds(PAD + HALO + cols, HALO), :
                ]

    fill(send_od, odd_x)
    fill(send_ev, jnp.logical_not(odd_x))


def first_kernel(dims, nsrc, meta, cur, *refs):
    res, vol, fx, fy, fz, wts, scl, one = tile_rows(dims, refs[: len(dims.tile)])
    two, rsd, cfc, gco, ins = refs[len(dims.tile) + 1 :]
    rows, halves = dims.rows, dims.halves
    weights = lambda x: [wts.at[k, x - 1] for k in range(6)]
    for x in range(2, rows - 2):
        sweep(dims, one.at[x - 2], one.at[x - 1], one.at[x], weights(x), two.at[x - 2])

    sources(
        dims, meta, cur, nsrc, range(2, rows - 2),
        lambda x, *rest: add_swept(two.at[x - 2], scl.at[x - 1], *rest),
    )

    for x in range(3, rows - 3):
        sweep(
            dims, two.at[x - 3], two.at[x - 2], two.at[x - 1], weights(x), rsd.at[x - 3],
            scl.at[x - 1],
        )

    def fix_rsd(row, col, h, amount):
        rsd[row - 3, h, pl.ds(col, 1), :] += amount

    sources(dims, meta, cur, nsrc, range(3, rows - 3), fix_rsd)

    both = [picker(dims, h, 0, 1) for h in range(halves)]
    even = [picker(dims, h, 0, 0) for h in range(halves)]
    n = dims.crows
    for c in range(n):
        pair = lambda row: [row(2 * c), row(2 * c + 1)]
        if c:
            cfc[c] = restrict(dims, [fx(2 * c)], 0, (0, 1), both)
        cfc[n + 1 + c] = restrict(dims, pair(fy), PAD, (0,), both)
        cfc[2 * n + 1 + c] = restrict(dims, pair(fz), 0, (0, 1), even)
        top = None
        for row in pair(res):
            for parity in (0, 1):
                part = face(row[halves - 1, pl.ds(PAD + parity, dims.cext, stride=2), :])
                top = part if top is None else top + part
        cfc[3 * n + 1 + c] = top
        ins[c] = res(2 * c)[0, pl.ds(PAD, dims.cext, stride=2), :]
    for c in range(1, n - 1):
        for k, part in enumerate(coarse_weights(dims, cfc, ins, c, cfc[c], cfc[c + 1])):
            gco[k, c - 1] = part


def coarse_weights(dims, cfc, ins, c, xl, xu):
    n = dims.crows
    lane = lanes_of(dims.cext)
    yl, zl = cfc[n + 1 + c], cfc[2 * n + 1 + c]
    yu = pltpu.roll(yl, dims.cext - 1, 0)
    zu = jnp.where(lane == LANES - 1, cfc[3 * n + 1 + c], pltpu.roll(zl, LANES - 1, 1))
    diag = xl + xu + yl + yu + zl + zu
    gain = jnp.where(ins[c] > 0, OMEGA / diag, 0.0)
    zl = jnp.where(lane == 0, 0.0, zl)
    zu = jnp.where(lane == LANES - 1, 0.0, zu)
    return [gain * part for part in (xl, xu, yl, yu, zl, zu)] + [gain]


def neighbours(rows):
    ext = rows.shape[0]
    return (
        pltpu.roll(rows, 1, 0),
        pltpu.roll(rows, ext - 1, 0),
        pltpu.roll(rows, 1, 1),
        pltpu.roll(rows, LANES - 1, 1),
    )


def coarse_side(field, base, weights):
    ylow, yhigh, zlow, zhigh = neighbours(field)
    return (
        (1.0 - OMEGA) * field
        + base
        + weights[YL] * ylow
        + weights[YU] * yhigh
        + weights[ZL] * zlow
        + weights[ZU] * zhigh
    )


def edge_sweep(dims, nsrc, meta, cur, res, vol, fx, fy, fz, hres, hvol, hfx, hfy, hfz, hwts, hscl,
               edge, regions, face_regions):
    rows = dims.rows
    last = rows - 1
    row_faces(dims, hres.at[1], hres.at[0], hfy.at[0], hfz.at[0], hfx.at[0], face_regions)
    row_faces(dims, res.at[0], hres.at[1], None, None, hfx.at[1], face_regions)
    row_faces(dims, hres.at[2], res.at[3], hfy.at[1], hfz.at[1], hfx.at[2], face_regions)
    row_faces(dims, hres.at[3], hres.at[2], None, None, hfx.at[3], face_regions)
    weights = lambda k: [hwts.at[j, k] for j in range(6)]
    for k, (row, xl, xu, yl, zl) in enumerate((
        (hres.at[1], hfx.at[0], hfx.at[1], hfy.at[0], hfz.at[0]),
        (res.at[0], hfx.at[1], fx.at[0], fy.at[0], fz.at[0]),
        (res.at[3], fx.at[1], hfx.at[2], fy.at[1], fz.at[1]),
        (hres.at[2], hfx.at[2], hfx.at[3], hfy.at[1], hfz.at[1]),
    )):
        row_weights(dims, row, xl, xu, yl, zl, weights(k), hscl.at[k], regions)
    for k, line in enumerate((
        (hvol.at[0], hvol.at[1], vol.at[0]),
        (hvol.at[1], vol.at[0], vol.at[1]),
        (vol.at[2], vol.at[3], hvol.at[2]),
        (vol.at[3], hvol.at[2], hvol.at[3]),
    )):
        sweep(dims, *line, weights(k), edge.at[k + 1], regions=regions)
    index = {-1: 0, 0: 1, last: 2, rows: 3}
    sources(
        dims, meta, cur, nsrc, (-1, 0, last, rows),
        lambda x, *rest: add_swept(edge.at[index[x] + 1], hscl.at[index[x]], *rest),
        regions,
    )


def edge_kernel(dims, nsrc, meta, cur, table, xod, xev, res, vol, fx, fy, fz, hres, hvol, hfx, hfy,
                hfz, hwts, hscl, edge):
    halves, cols = dims.halves, dims.cols
    odd_x = meta[3 * nsrc] == 1
    margin = PAD + HALO
    for side in range(2):
        choose = lambda a, b: jnp.where(odd_x, b, a) if side == 0 else jnp.where(odd_x, a, b)
        for k in range(2):
            for h in range(halves):
                lanes = slice(h * LANES, (h + 1) * LANES)
                zero = jnp.zeros((margin, LANES), F32)
                for ref in (hres, hvol):
                    ref[2 * side + k, h, pl.ds(0, margin), :] = zero
                    ref[2 * side + k, h, pl.ds(margin + cols, margin), :] = zero
                wide = pl.ds(margin, cols)
                hvol[2 * side + k, h, wide, :] = choose(xod[k, :, lanes], xev[k, :, lanes])
                number = choose(xod[2 + k, :, lanes], xev[2 + k, :, lanes]).astype(jnp.int32)
                hres[2 * side + k, h, wide, :] = jnp.where(
                    number > 0, lookup(number - 1, table), 0.0
                )
        for h in range(halves):
            hfy[side, h, pl.ds(PAD + dims.ext, PAD), :] = jnp.zeros((PAD, LANES), F32)
    edge_sweep(dims, nsrc, meta, cur, res, vol, fx, fy, fz, hres, hvol, hfx, hfy, hfz, hwts, hscl,
               edge, dims.inside, [(HALO, cols)])


def second_kernel(dims, nsrc, meta, cur, sod, sev, wts, scl, one, two, rsd, res, vol, fx, fy, fz,
                  cfc, gci, ins, *refs):
    rows, halves, cols = dims.rows, dims.halves, dims.cols
    hres, hvol, hfx, hfy, hfz, hwts, hscl, edge, htwo, gco, base, c_od, c_ev, v_od, v_ev, redge = (
        refs[8:]
    )
    odd_x = meta[3 * nsrc] == 1
    last = rows - 1
    for side in range(2):
        choose = lambda a, b: jnp.where(odd_x, b, a) if side == 0 else jnp.where(odd_x, a, b)
        for h in range(halves):
            for k in range(2):
                for ref, kind in ((hvol, k), (hres, 2 + k)):
                    strip = halves * dims.ext + (kind * halves + h) * 2 * HALO
                    low = pl.ds(strip, HALO)
                    high = pl.ds(strip + HALO, HALO)
                    ref[2 * side + k, h, pl.ds(PAD, HALO), :] = choose(sod[low, :], sev[low, :])
                    ref[2 * side + k, h, pl.ds(PAD + HALO + cols, HALO), :] = choose(
                        sod[high, :], sev[high, :]
                    )
            span = pl.ds(h * dims.ext, dims.ext)
            edge[5 * side, h, pl.ds(PAD, dims.ext), :] = choose(sod[span, :], sev[span, :])
    edge_sweep(dims, nsrc, meta, cur, res, vol, fx, fy, fz, hres, hvol, hfx, hfy, hfz, hwts, hscl,
               edge, dims.strips, dims.strips)

    outer = lambda x: x + 1 if x <= 0 else x - last + 2
    inner = lambda x: 1 <= x <= last - 1
    weights = lambda x: [
        wts.at[k, x - 1] if inner(x) else hwts.at[k, outer(x)] for k in range(6)
    ]
    scale = lambda x: scl.at[x - 1] if inner(x) else hscl.at[outer(x)]

    def swept(x):
        if x <= 0:
            return edge.at[x + 2]
        return one.at[x - 1] if x < last else edge.at[x - last + 3]

    def twice(x):
        if x <= 1:
            return htwo.at[x + 1]
        return two.at[x - 2] if x < last - 1 else htwo.at[x - last + 4]

    for x in (-1, 0, 1, last - 1, last, rows):
        sweep(dims, swept(x - 1), swept(x), swept(x + 1), weights(x), twice(x))
    sources(
        dims, meta, cur, nsrc, (-1, 0, 1, last - 1, last, rows),
        lambda x, *rest: add_swept(twice(x), scale(x), *rest),
    )
    pick_od = jnp.where(odd_x, 3, 2)
    pick_ev = jnp.where(odd_x, 2, 3)
    for h in range(halves):
        v_od[h, :, :] = htwo[pick_od, h, pl.ds(PAD, dims.ext), :]
        v_ev[h, :, :] = htwo[pick_ev, h, pl.ds(PAD, dims.ext), :]

    def resid_row(x):
        if x <= 2:
            return redge.at[x]
        return rsd.at[x - 3] if x < last - 2 else redge.at[x - last + 5]

    for x in (0, 1, 2, last - 2, last - 1, last):
        sweep(
            dims, twice(x - 1), twice(x), twice(x + 1), weights(x), resid_row(x), scale(x)
        )

    def fix_rsd(x, col, h, amount):
        resid_row(x)[h, pl.ds(col, 1), :] += amount

    sources(dims, meta, cur, nsrc, (0, 1, 2, last - 2, last - 1, last), fix_rsd)

    both = [picker(dims, h, 0, 1) for h in range(halves)]
    n = dims.crows
    bottom = restrict(dims, [hfx.at[1]], 0, (0, 1), both)
    topmost = restrict(dims, [hfx.at[2]], 0, (0, 1), both)

    e1, gc = [], []
    for c in range(n):
        total = restrict(dims, [resid_row(2 * c), resid_row(2 * c + 1)], 0, (0, 1), both)
        if 0 < c < n - 1:
            parts = [gci[k, c - 1] for k in range(7)]
        else:
            xl = bottom if c == 0 else cfc[c]
            xu = topmost if c == n - 1 else cfc[c + 1]
            parts = coarse_weights(dims, cfc, ins, c, xl, xu)
            for k in range(6):
                gco[k, 0 if c == 0 else 1] = parts[k]
        gc.append(parts)
        e1.append(parts[6] * total)
        base[c] = e1[c]

    low = (e1[0], coarse_side(e1[0], e1[0], gc[0]) + gc[0][XU] * e1[1], gc[0][XL])
    high = (
        e1[n - 1],
        coarse_side(e1[n - 1], e1[n - 1], gc[n - 1]) + gc[n - 1][XL] * e1[n - 2],
        gc[n - 1][XU],
    )
    for k in range(3):
        c_od[k] = jnp.where(odd_x, high[k], low[k])
        c_ev[k] = jnp.where(odd_x, low[k], high[k])


def coarse_row(dims, gci, gco, c):
    if 0 < c < dims.crows - 1:
        return [gci[k, c - 1] for k in range(6)]
    return [gco[k, 0 if c == 0 else 1] for k in range(6)]


def third_kernel(dims, nsrc, meta, gci, gco, base, rod, rev, e3, c_od, c_ev):
    n = dims.crows
    odd_x = meta[3 * nsrc] == 1
    low = [jnp.where(odd_x, rev[k], rod[k]) for k in range(3)]
    high = [jnp.where(odd_x, rod[k], rev[k]) for k in range(3)]
    gc = lambda c: coarse_row(dims, gci, gco, c)

    def coarse_sweep(field, under, over):
        out = []
        for c in range(n):
            w = gc(c)
            new = coarse_side(field[c], base[c], w)
            new += w[XL] * (field[c - 1] if c else under)
            new += w[XU] * (field[c + 1] if c < n - 1 else over)
            out.append(new)
        return out

    e1 = [base[c] for c in range(n)]
    e2 = coarse_sweep(e1, low[0], high[0])
    under = low[1] + low[2] * e1[0]
    over = high[1] + high[2] * e1[n - 1]
    out = coarse_sweep(e2, under, over)
    for c in range(n):
        e3[c] = out[c]
    w = gc(0)
    first = (out[0], coarse_side(out[0], base[0], w) + w[XU] * out[1])
    w = gc(n - 1)
    final = (out[n - 1], coarse_side(out[n - 1], base[n - 1], w) + w[XL] * out[n - 2])
    for k in range(2):
        c_od[k] = jnp.where(odd_x, final[k], first[k])
        c_ev[k] = jnp.where(odd_x, first[k], final[k])


def fourth_kernel(dims, nsrc, meta, cur, gci, gco, base, e3, rod, rev, tod, tev, vod, vev, wts, scl,
                  two, hwts, hscl, htwo, out, raised, zero, three, done, sems):
    rows, halves, cols = dims.rows, dims.halves, dims.cols
    n = dims.crows
    odd_x = meta[3 * nsrc] == 1
    below_of = lambda od, ev: jnp.where(odd_x, ev, od)
    above_of = lambda od, ev: jnp.where(odd_x, od, ev)
    field = [e3[c] for c in range(n)]
    under = below_of(tod[1], tev[1]) + below_of(rod[2], rev[2]) * field[0]
    over = above_of(tod[1], tev[1]) + above_of(rod[2], rev[2]) * field[n - 1]
    e4 = [under]
    for c in range(n):
        w = coarse_row(dims, gci, gco, c)
        new = coarse_side(field[c], base[c], w)
        new += w[XL] * (field[c - 1] if c else below_of(tod[0], tev[0]))
        new += w[XU] * (field[c + 1] if c < n - 1 else above_of(tod[0], tev[0]))
        e4.append(new)
    e4.append(over)
    spread = []
    for h in range(halves):
        fine = lax.broadcasted_iota(jnp.int32, (LANES, LANES), 1) + h * LANES
        coarse = lax.broadcasted_iota(jnp.int32, (LANES, LANES), 0)
        hit = (fine >= 2 * coarse) & (fine <= 2 * coarse + 1)
        spread.append(jnp.where(hit, 1.0, 0.0).astype(jnp.bfloat16))
    for c in range(n + 2):
        for h in range(halves):
            lifted = split_dot(e4[c], spread[h])
            raised[c, h, pl.ds(0, dims.cext, stride=2), :] = lifted
            raised[c, h, pl.ds(1, dims.cext, stride=2), :] = lifted

    last = rows - 1

    def twice(x):
        if x <= 1:
            return htwo.at[x + 1]
        return two.at[x - 2] if x < last - 1 else htwo.at[x - last + 4]

    outer = lambda x: x + 1 if x <= 0 else x - last + 2
    inner = lambda x: 1 <= x <= last - 1
    weights = lambda x: [
        wts.at[k, x - 1] if inner(x) else hwts.at[k, outer(x)] for k in range(6)
    ]
    scale = lambda x: scl.at[x - 1] if inner(x) else hscl.at[outer(x)]
    for x in range(-2, rows + 2):
        for h in range(halves):
            wide = pl.ds(PAD, dims.ext)
            if x == -2:
                value = below_of(vod[h, :, :], vev[h, :, :])
            elif x == rows + 1:
                value = above_of(vod[h, :, :], vev[h, :, :])
            else:
                value = twice(x)[h, wide, :]
            zero[x + 2, h, wide, :] = value + raised[(x + 2) // 2, h, :, :]
    for x in range(-1, rows + 1):
        sweep(dims, zero.at[x + 1], zero.at[x + 2], zero.at[x + 3], weights(x), three.at[x + 1])
    sources(
        dims, meta, cur, nsrc, range(-1, rows + 1),
        lambda x, *rest: add_swept(three.at[x + 1], scale(x), *rest),
    )
    copies = []
    for x in range(rows):
        last_sweep(
            dims, nsrc, meta, cur, x, three.at[x], three.at[x + 1], three.at[x + 2], weights(x),
            scale(x), done.at[x],
        )
        copy = pltpu.make_async_copy(done.at[x], out.at[x], sems.at[x])
        copy.start()
        copies.append(copy)
    for copy in copies:
        copy.wait()


def last_sweep(dims, nsrc, meta, cur, x, below_row, row, above_row, w, scale, done):
    halves = dims.halves

    at, size = PAD + HALO, dims.cols
    here = [row[h, pl.ds(at, size), :] for h in range(halves)]
    zlow, zhigh = below(here), above(here)
    for h in range(halves):
        span = pl.ds(HALO, size)
        acc = w[XL][h, span, :] * below_row[h, pl.ds(at, size), :]
        acc += w[XU][h, span, :] * above_row[h, pl.ds(at, size), :]
        acc += w[YL][h, span, :] * row[h, pl.ds(at - 1, size), :]
        acc += w[YU][h, span, :] * row[h, pl.ds(at + 1, size), :]
        acc += w[ZL][h, span, :] * zlow[h]
        acc += w[ZU][h, span, :] * zhigh[h]
        done[:, h * LANES : (h + 1) * LANES] = acc + (1.0 - OMEGA) * here[h]
    for s in range(nsrc):
        r, col, dep = meta[s], meta[nsrc + s], meta[2 * nsrc + s]

        @pl.when((r == x) & (col >= 0) & (col < dims.cols))
        def _():
            for h in range(halves):
                block = pl.multiple_of(col // 8 * 8, 8)
                place = lax.broadcasted_iota(jnp.int32, (8, LANES), 0) + block
                hit = (lanes_of(8) == dep - h * LANES) & (place == col)
                amount = jnp.where(hit, cur[s], 0.0)
                done[pl.ds(block, 8), h * LANES : (h + 1) * LANES] += (
                    amount / scale[h, pl.ds(block + HALO, 8), :]
                )


def call(kernel, outs, ins, specs, scratch=(), aliases=None, out_specs=None, limit=24, cost=1):
    return pl.pallas_call(
        kernel,
        out_shape=[jax.ShapeDtypeStruct(shape, F32) for shape in outs],
        in_specs=specs,
        out_specs=out_specs if out_specs is not None else [VM] * len(outs),
        scratch_shapes=list(scratch),
        input_output_aliases=aliases or {},
        compiler_params=pltpu.CompilerParams(vmem_limit_bytes=limit * 2**20),
        cost_estimate=pl.CostEstimate(flops=cost, bytes_accessed=cost, transcendentals=0),
    )(*ins)


def swaps(count):
    pairs = []
    for first in (1, 0):
        found = []
        for low in range(first, count - 1, 2):
            found += [(low, low + 1), (low + 1, low)]
        pairs.append(found)
    return pairs


def swap(od, ev, axis):
    odd_pairs, even_pairs = swaps(lax.axis_size(axis))
    return lax.ppermute(od, axis, odd_pairs), lax.ppermute(ev, axis, even_pairs)


def per_device(potential, classes, sigma_table, row_index, col_index, depth_index, currents):
    dims = Dims(potential.shape)
    rows, cols, depth = potential.shape
    halves, ext, padded, n, cext = dims.halves, dims.ext, dims.padded, dims.crows, dims.cext
    nsrc = row_index.shape[0]
    gx, gy = lax.axis_index("gx"), lax.axis_index("gy")
    odd_x, odd_y = gx % 2, gy % 2
    meta = jnp.concatenate(
        [
            row_index - gx * rows,
            col_index - gy * cols,
            depth_index,
            jnp.stack([odd_x, odd_y]),
        ]
    ).astype(jnp.int32)
    table = 1.0 / sigma_table

    bind = lambda kernel: functools.partial(kernel, dims, nsrc)
    wide = lambda k: (k, halves, padded, LANES)
    flat = lambda k: (k, halves, ext, LANES)
    send = (halves * ext + 4 * halves * 2 * HALO, LANES)
    coarse = lambda *k: (*k, cext, LANES)
    vmem = lambda *shapes: [pltpu.VMEM(shape, F32) for shape in shapes]
    hbm = pl.BlockSpec(memory_space=pl.ANY)
    far = pl.BlockSpec(memory_space=pltpu.HBM)

    def edges(kernel, shape, kept):
        return call(
            kernel, [shape] * 2, [potential, classes], [far] * 2,
            scratch=[pltpu.VMEM((2, *kept), jnp.int32), pltpu.SemaphoreType.DMA((2, 2))],
            limit=54,
        )

    xod, xev = swap(*edges(x_edge_kernel, (4, cols, depth), (2, cols, depth)), "gx")
    yod, yev = swap(
        *edges(y_edge_kernel, (2, rows, HALO, depth), (rows, HALO, depth)), "gy"
    )
    tile = dims.tile = [
        wide(4), wide(4), flat(2), wide(2), flat(2), wide(rows - 4), wide(rows - 4),
        flat(rows - 3), wide(rows - 2), flat(rows - 2), (6, *flat(rows - 2)), flat(rows - 2),
        wide(rows - 2),
    ]
    parts = call(
        bind(tile_kernel), tile, [meta, currents, table, potential, classes],
        [SM] * 3 + [VM] * 2,
        limit=4,
    )
    parts = call(
        bind(strip_kernel),
        tile + [send, send],
        [meta, currents, table, yod, yev, *parts],
        [SM] * 3 + [VM] * (2 + len(tile)),
        aliases={5 + k: k for k in range(len(tile))},
        limit=4,
    )
    res, vol, fx, fy, fz = parts[:5]
    wts, scl, one, s_od, s_ev = parts[10:]
    sod, sev = swap(s_od, s_ev, "gx")
    (two, rsd, cfc, gci, ins) = call(
        bind(first_kernel),
        [wide(rows - 4), flat(rows - 6), coarse(4 * n + 1), coarse(7, n - 2), coarse(n)],
        [meta, currents, *parts[: len(tile) + 1]],
        [SM] * 2 + [VM] * (len(tile) + 1),
        limit=4,
    )
    held = [wide(4), wide(4), flat(4), wide(2), flat(2), (6, *flat(4)), flat(4), wide(6)]
    edges = call(
        bind(edge_kernel),
        held,
        [meta, currents, table, xod, xev, res, vol, fx, fy, fz],
        [SM] * 3 + [VM] * 7,
        limit=4,
    )
    ins_of = [meta, currents, sod, sev, wts, scl, one, two, rsd, res, vol, fx, fy, fz, cfc, gci, ins]
    outs = call(
        bind(second_kernel),
        held + [wide(6), coarse(6, 2), coarse(n), coarse(3), coarse(3)] + [flat(1)[1:]] * 2,
        ins_of + list(edges),
        [SM] * 2 + [VM] * (len(ins_of) - 2 + len(held)),
        scratch=vmem(flat(6)),
        aliases={len(ins_of) + k: k for k in range(len(held))},
        limit=4,
    )
    hwts, hscl, (htwo, gco, base, c_od, c_ev, v_od, v_ev) = outs[5], outs[6], outs[8:]
    rod, rev = swap(c_od, c_ev, "gx")
    vod, vev = swap(v_od, v_ev, "gx")
    (e3, t_od, t_ev) = call(
        bind(third_kernel),
        [coarse(n), coarse(2), coarse(2)],
        [meta, gci, gco, base, rod, rev],
        [SM] + [VM] * 5,
        limit=4,
    )
    tod, tev = swap(t_od, t_ev, "gx")
    (out,) = call(
        bind(fourth_kernel),
        [(rows, cols, depth)],
        [meta, currents, gci, gco, base, e3, rod, rev, tod, tev, vod, vev, wts, scl, two, hwts,
         hscl, htwo],
        [SM] * 2 + [VM] * 16,
        scratch=vmem(flat(n + 2), wide(rows + 4), wide(rows + 2), (rows, cols, depth))
        + [pltpu.SemaphoreType.DMA((rows,))],
        out_specs=[hbm],
        limit=13,
    )
    return out


def solution(mesh):
    tiled = P("gx", "gy", None)
    return jax.shard_map(
        per_device,
        mesh=mesh,
        in_specs=(tiled, tiled, P(), P(), P(), P(), P()),
        out_specs=tiled,
        check_vma=False,
    )
```

```python
import functools

import jax
import jax.numpy as jnp
from jax import lax
from jax.experimental import pallas as pl
from jax.experimental.pallas import tpu as pltpu
from jax.sharding import PartitionSpec as P

OMEGA = 0.8
HALO = 16
CORNER = 12
GROUP = 4
TRIM = 8
STEP = 16
PAD = 8
LANES = 128
F32 = jnp.float32
XL, XU, YL, YU, ZL, ZU = range(6)

VM = pl.BlockSpec(memory_space=pltpu.VMEM)
SM = pl.BlockSpec(memory_space=pltpu.SMEM)


class Dims:
    def __init__(self, shape):
        self.rows, self.cols, self.depth = shape
        self.halves = self.depth // LANES
        self.ext = self.cols + 2 * HALO
        self.padded = self.ext + 2 * PAD
        self.crows = self.rows // 2
        self.cext = self.ext // 2
        self.whole = [(0, self.ext)]
        side = HALO + PAD
        self.inside = [(side, self.ext - 2 * side)]
        self.strips = [(0, side), (self.ext - side, side)]

    def within(self, margin):
        return [(margin, self.ext - 2 * margin)]

    def beside(self, margin):
        return [(0, margin), (self.ext - margin, margin)]


def lanes_of(rows):
    return lax.broadcasted_iota(jnp.int32, (rows, LANES), 1)


def below(parts):
    return [pltpu.roll(parts[1], 1, 1), parts[0]]


def above(parts):
    return [parts[1], pltpu.roll(parts[0], LANES - 1, 1)]


def depth_shuffle(depth, back=False):
    left = lax.broadcasted_iota(jnp.int32, (depth, depth), 0)
    right = lax.broadcasted_iota(jnp.int32, (depth, depth), 1)
    if back:
        left, right = right, left
    target = jnp.where(left % 2 == 0, left // 2, depth // 2 + left // 2)
    return jnp.where(right == target, 1.0, 0.0).astype(jnp.bfloat16)


def face(total):
    return jnp.where(total > 0, 2.0 / total, 0.0)


def lookup(cells, table):
    bits = [(cells & (1 << b)) != 0 for b in range(3)]
    level = [table[k] for k in range(8)]
    for bit in bits:
        level = [jnp.where(bit, level[k + 1], level[k]) for k in range(0, len(level), 2)]
    return level[0]


def sweep(dims, get, targets, weights, out, scale=None, regions=None):
    for y0, size in regions or dims.whole:
        for at in range(y0, y0 + size, STEP):
            width = min(STEP, y0 + size - at)
            span, wide = pl.ds(at, width), pl.ds(at + PAD, width)
            held = {}

            def value(x):
                if x not in held:
                    held[x] = [get(x)[h, wide, :] for h in range(dims.halves)]
                return held[x]

            for x in targets:
                here, w = value(x), weights(x)
                zlow, zhigh = below(here), above(here)
                for h in range(dims.halves):
                    acc = w[XL][h, span, :] * value(x - 1)[h]
                    acc += w[XU][h, span, :] * value(x + 1)[h]
                    acc += w[YL][h, span, :] * get(x)[h, pl.ds(at + PAD - 1, width), :]
                    acc += w[YU][h, span, :] * get(x)[h, pl.ds(at + PAD + 1, width), :]
                    acc += w[ZL][h, span, :] * zlow[h]
                    acc += w[ZU][h, span, :] * zhigh[h]
                    if scale is None:
                        out(x)[h, wide, :] = acc + (1.0 - OMEGA) * here[h]
                    else:
                        out(x)[h, span, :] = (acc - OMEGA * here[h]) * scale(x)[h, span, :]


def sources(dims, meta, cur, count, targets, fix, regions=None):
    spots = []
    anywhere = None
    for s in range(count):
        row, ext_col = meta[s], meta[count + s] + HALO
        held = None
        for y0, size in regions or dims.whole:
            hit = (ext_col >= y0) & (ext_col < y0 + size)
            held = hit if held is None else held | hit
        held = (row >= targets[0]) & (row <= targets[-1]) & held
        anywhere = held if anywhere is None else anywhere | held
        spots.append((s, row, ext_col, held))

    @pl.when(anywhere)
    def _():
        for s, row, ext_col, held in spots:
            for x in targets:

                @pl.when(held & (row == x))
                def _(s=s, ext_col=ext_col, x=x):
                    for h in range(dims.halves):
                        hit = 2 * lanes_of(1) + h == meta[2 * count + s]
                        fix(x, ext_col, h, jnp.where(hit, cur[s], 0.0))


def add_swept(field, scale, col, h, amount):
    field[h, pl.ds(col + PAD, 1), :] += amount / scale[h, pl.ds(col, 1), :]


def row_faces(dims, row, row_below, yl_out, zl_out, xl_out, regions=None):
    for y0, size in regions or dims.whole:
        span, wide = pl.ds(y0, size), pl.ds(y0 + PAD, size)
        here = [row[h, wide, :] for h in range(dims.halves)]
        zlow = below(here)
        zlow[0] = jnp.where(lanes_of(size) == 0, 0.0, zlow[0])
        for h in range(dims.halves):
            if xl_out is not None:
                xl_out[h, span, :] = face(here[h] + row_below[h, wide, :])
            if yl_out is not None:
                yl_out[h, wide, :] = face(here[h] + row[h, pl.ds(y0 + PAD - 1, size), :])
                zl_out[h, span, :] = face(here[h] + zlow[h])


def row_weights(dims, row, xl, xu, yl, zl, weights, scale, regions=None):
    for y0, size in regions or dims.whole:
        span, wide = pl.ds(y0, size), pl.ds(y0 + PAD, size)
        low = [zl[h, span, :] for h in range(dims.halves)]
        high = above(low)
        lane = lanes_of(size)
        top = dims.halves - 1
        high[top] = jnp.where(lane == LANES - 1, face(row[top, wide, :]), high[top])
        for h in range(dims.halves):
            parts = [
                xl[h, span, :],
                xu[h, span, :],
                yl[h, wide, :],
                yl[h, pl.ds(y0 + PAD + 1, size), :],
                low[h],
                high[h],
            ]
            diag = parts[0] + parts[1] + parts[2] + parts[3] + parts[4] + parts[5]
            gain = jnp.where(row[h, wide, :] > 0, OMEGA / diag, 0.0)
            scale[h, span, :] = diag * (1.0 / OMEGA)
            if h == 0:
                parts[ZL] = jnp.where(lane == 0, 0.0, parts[ZL])
            if h == top:
                parts[ZU] = jnp.where(lane == LANES - 1, 0.0, parts[ZU])
            for k in range(6):
                weights[k][h, span, :] = gain * parts[k]


def split_dot(field, chosen, pieces=2):
    total = None
    for _ in range(pieces):
        piece = field.astype(jnp.bfloat16)
        field = field - piece.astype(F32)
        term = jnp.dot(piece, chosen, preferred_element_type=F32)
        total = term if total is None else total + term
    return total


def restrict(dims, rows, offset, parities, parts=(0, 1)):
    total = None
    for h in parts:
        for row in rows:
            for parity in parities:
                part = row[h, pl.ds(offset + parity, dims.cext, stride=2), :]
                total = part if total is None else total + part
    return total


def edge_message(axis, dim, width, wanted, pot, cls, out, kept, sems):
    high = lax.axis_index(axis) % 2 == wanted
    start = jnp.where(high, pot.shape[dim] - width, 0)
    if dim == 0:
        at, pot_out, cls_out = pl.ds(start, width), out.at[pl.ds(0, width)], pl.ds(width, width)
    else:
        at = (slice(None), pl.ds(pl.multiple_of(start, 8), width))
        pot_out, cls_out = out.at[0], 1
    copies = [
        pltpu.make_async_copy(cls.at[at], kept, sems.at[0]),
        pltpu.make_async_copy(pot.at[at], pot_out, sems.at[1]),
    ]
    for copy in copies:
        copy.start()
    copies[0].wait()
    out[cls_out] = kept[...].astype(F32) + 1.0
    copies[1].wait()


def tile_rows(dims, refs):
    rows = dims.rows
    ends, pairs = [0, rows - 1], [0, 1, rows - 2, rows - 1]
    edges = [pairs, pairs, [1, rows - 1], ends, ends]

    def getter(edge, middle, named, first):
        others = [x for x in range(first, rows) if x not in named]
        return lambda x: edge.at[named.index(x)] if x in named else middle.at[others.index(x)]

    found = [getter(refs[k], refs[5 + k], edges[k], int(k == 2)) for k in range(5)]
    return found + list(refs[10:13])


def own_rows(dims, nsrc, meta, cur, res, vol, fx, fy, fz, wts, scl, one, regions, face_regions):
    rows = dims.rows
    for x in range(rows):
        row_faces(
            dims,
            res(x),
            res(x - 1) if x else None,
            fy(x),
            fz(x),
            fx(x) if x else None,
            face_regions,
        )
    weights = lambda x: [wts.at[k, x - 1] for k in range(6)]
    for x in range(1, rows - 1):
        row_weights(
            dims, res(x), fx(x), fx(x + 1), fy(x), fz(x), weights(x),
            scl.at[x - 1], regions,
        )
    sweep(dims, vol, range(1, rows - 1), weights, lambda x: one.at[x - 1], regions=regions)
    sources(
        dims, meta, cur, nsrc, range(1, rows - 1),
        lambda x, *rest: add_swept(one.at[x - 1], scl.at[x - 1], *rest),
        regions,
    )


def tile_kernel(dims, nsrc, meta, cur, table, pot, cls, *refs):
    res, vol, fx, fy, fz, wts, scl, one = tile_rows(dims, refs)
    margin = PAD + HALO
    shuffle = depth_shuffle(dims.depth)
    for x in range(dims.rows):
        field = split_dot(pot[x], shuffle)
        number = split_dot(cls[x].astype(F32), shuffle, 1).astype(jnp.int32)
        for h in range(dims.halves):
            lanes = slice(h * LANES, (h + 1) * LANES)
            zero = jnp.zeros((margin, LANES), F32)
            for ref in (res, vol):
                ref(x)[h, pl.ds(0, margin), :] = zero
                ref(x)[h, pl.ds(margin + dims.cols, margin), :] = zero
            vol(x)[h, pl.ds(margin, dims.cols), :] = field[:, lanes]
            res(x)[h, pl.ds(margin, dims.cols), :] = lookup(number[:, lanes], table)
    own_rows(dims, nsrc, meta, cur, res, vol, fx, fy, fz, wts, scl, one, dims.inside,
             [(HALO, dims.cols)])


def strip_kernel(dims, nsrc, meta, cur, table, yod, yev, *refs):
    count = len(dims.tile)
    res_edge, vol_edge = refs[count], refs[count + 1]
    res, vol, fx, fy, fz, wts, scl, one = tile_rows(dims, refs[count : 2 * count])
    send_od, send_ev = refs[2 * count :]
    rows, halves, cols = dims.rows, dims.halves, dims.cols
    odd_x, odd_y = meta[3 * nsrc] == 1, meta[3 * nsrc + 1] == 1
    shuffle = depth_shuffle(dims.depth)
    for into, take_ev in ((PAD, True), (PAD + HALO + cols, False)):
        pair = []
        for k in range(2):
            a, b = yod[k], yev[k]
            chosen = jnp.where(odd_y, b, a) if take_ev else jnp.where(odd_y, a, b)
            chosen = chosen.reshape(rows * HALO, dims.depth)
            pair.append(split_dot(chosen, shuffle, 1 if k else 2))
        number = pair[1].astype(jnp.int32)
        inverse = jnp.where(number > 0, lookup(number - 1, table), 0.0)
        for x in range(rows):
            at = slice(x * HALO, (x + 1) * HALO)
            for h in range(halves):
                lanes = slice(h * LANES, (h + 1) * LANES)
                vol(x)[h, pl.ds(into, HALO), :] = pair[0][at, lanes]
                res(x)[h, pl.ds(into, HALO), :] = inverse[at, lanes]
    for x in range(rows):
        for h in range(halves):
            fy(x)[h, pl.ds(PAD + dims.ext, PAD), :] = jnp.zeros((PAD, LANES), F32)
    own_rows(dims, nsrc, meta, cur, res, vol, fx, fy, fz, wts, scl, one, dims.strips, dims.strips)

    def fill(send, high):
        edge = jnp.where(high, 2, 0)
        inner = jnp.where(high, rows - 2, 1)
        for h in range(halves):
            send[pl.ds(h * dims.ext, dims.ext), :] = one[inner - 1, h, pl.ds(PAD, dims.ext), :]
        base = halves * dims.ext
        for k in range(4):
            ref = vol_edge if k < 2 else res_edge
            for h in range(halves):
                at = base + (k * halves + h) * 2 * CORNER
                send[pl.ds(at, CORNER), :] = ref[
                    edge + k % 2, h, pl.ds(PAD + HALO - CORNER, CORNER), :
                ]
                send[pl.ds(at + CORNER, CORNER), :] = ref[
                    edge + k % 2, h, pl.ds(PAD + HALO + cols, CORNER), :
                ]

    fill(send_od, odd_x)
    fill(send_ev, jnp.logical_not(odd_x))


def first_kernel(dims, nsrc, meta, cur, *refs):
    res, vol, fx, fy, fz, wts, scl, one = tile_rows(dims, refs[: len(dims.tile)])
    two, rsd, ced, gco, ins, cfc = refs[len(dims.tile) + 1 :]
    rows, halves = dims.rows, dims.halves
    weights = lambda x: [wts.at[k, x - 1] for k in range(6)]
    sweep(
        dims, lambda x: one.at[x - 1], range(2, rows - 2), weights, lambda x: two.at[x - 2]
    )

    sources(
        dims, meta, cur, nsrc, range(2, rows - 2),
        lambda x, *rest: add_swept(two.at[x - 2], scl.at[x - 1], *rest),
    )

    sweep(
        dims, lambda x: two.at[x - 2], range(3, rows - 3), weights, lambda x: rsd.at[x - 3],
        lambda x: scl.at[x - 1],
    )

    def fix_rsd(row, col, h, amount):
        rsd[row - 3, h, pl.ds(col, 1), :] += amount

    sources(dims, meta, cur, nsrc, range(3, rows - 3), fix_rsd)

    n = dims.crows
    for c in range(n):
        pair = lambda row: [row(2 * c), row(2 * c + 1)]
        if c:
            cfc[c] = restrict(dims, [fx(2 * c)], 0, (0, 1))
        cfc[n + 1 + c] = restrict(dims, pair(fy), PAD, (0,))
        cfc[2 * n + 1 + c] = restrict(dims, pair(fz), 0, (0, 1), (0,))
        top = None
        for row in pair(res):
            for parity in (0, 1):
                part = face(row[halves - 1, pl.ds(PAD + parity, dims.cext, stride=2), :])
                top = part if top is None else top + part
        cfc[3 * n + 1 + c] = top
        ins[c] = res(2 * c)[0, pl.ds(PAD, dims.cext, stride=2), :]
    for c in range(1, n - 1):
        kinds = [cfc[c], cfc[c + 1]] + [cfc[j * n + 1 + c] for j in (1, 2, 3)]
        for k, part in enumerate(coarse_weights(dims, ins[c], *kinds)):
            gco[k, c - 1] = part
    for side, c in enumerate((0, n - 1)):
        ced[4 * side] = cfc[1 if c == 0 else n - 1]
        for k in range(3):
            ced[4 * side + 1 + k] = cfc[(k + 1) * n + 1 + c]


def coarse_weights(dims, inside, xl, xu, yl, zl, top):
    lane = lanes_of(dims.cext)
    yu = pltpu.roll(yl, dims.cext - 1, 0)
    zu = jnp.where(lane == LANES - 1, top, pltpu.roll(zl, LANES - 1, 1))
    diag = xl + xu + yl + yu + zl + zu
    gain = jnp.where(inside > 0, OMEGA / diag, 0.0)
    zl = jnp.where(lane == 0, 0.0, zl)
    zu = jnp.where(lane == LANES - 1, 0.0, zu)
    return [gain * part for part in (xl, xu, yl, yu, zl, zu)] + [gain]


def neighbours(rows):
    ext = rows.shape[0]
    return (
        pltpu.roll(rows, 1, 0),
        pltpu.roll(rows, ext - 1, 0),
        pltpu.roll(rows, 1, 1),
        pltpu.roll(rows, LANES - 1, 1),
    )


def coarse_side(field, base, weights):
    ylow, yhigh, zlow, zhigh = neighbours(field)
    return (
        (1.0 - OMEGA) * field
        + base
        + weights[YL] * ylow
        + weights[YU] * yhigh
        + weights[ZL] * zlow
        + weights[ZU] * zhigh
    )


def edge_sweep(dims, nsrc, meta, cur, res, vol, fx, fy, fz, hres, hvol, hfx, hfy, hfz, hwts, hscl,
               edge, regions, face_regions):
    rows = dims.rows
    last = rows - 1
    row_faces(dims, hres.at[1], hres.at[0], hfy.at[0], hfz.at[0], hfx.at[0], face_regions)
    row_faces(dims, res.at[0], hres.at[1], None, None, hfx.at[1], face_regions)
    row_faces(dims, hres.at[2], res.at[3], hfy.at[1], hfz.at[1], hfx.at[2], face_regions)
    row_faces(dims, hres.at[3], hres.at[2], None, None, hfx.at[3], face_regions)
    weights = lambda k: [hwts.at[j, k] for j in range(6)]
    for k, (row, xl, xu, yl, zl) in enumerate((
        (hres.at[1], hfx.at[0], hfx.at[1], hfy.at[0], hfz.at[0]),
        (res.at[0], hfx.at[1], fx.at[0], fy.at[0], fz.at[0]),
        (res.at[3], fx.at[1], hfx.at[2], fy.at[1], fz.at[1]),
        (hres.at[2], hfx.at[2], hfx.at[3], hfy.at[1], hfz.at[1]),
    )):
        row_weights(dims, row, xl, xu, yl, zl, weights(k), hscl.at[k], regions)
    index = {-1: 0, 0: 1, last: 2, rows: 3}

    def start(x):
        if x < 0:
            return hvol.at[x + 2]
        if x >= rows:
            return hvol.at[x - rows + 2]
        return vol.at[x if x <= 1 else x - last + 3]

    for pair in ((-1, 0), (last, rows)):
        sweep(
            dims, start, pair, lambda x: weights(index[x]), lambda x: edge.at[index[x] + 1],
            regions=regions,
        )
    sources(
        dims, meta, cur, nsrc, (-1, 0, last, rows),
        lambda x, *rest: add_swept(edge.at[index[x] + 1], hscl.at[index[x]], *rest),
        regions,
    )


def edge_rows(dims, wts, scl, one, two, rsd, hwts, hscl, edge, htwo, redge):
    last = dims.rows - 1
    outer = lambda x: x + 1 if x <= 0 else x - last + 2
    inner = lambda x: 1 <= x <= last - 1
    weights = lambda x: [
        wts.at[k, x - 1] if inner(x) else hwts.at[k, outer(x)] for k in range(6)
    ]
    scale = lambda x: scl.at[x - 1] if inner(x) else hscl.at[outer(x)]

    def swept(x):
        if x <= 0:
            return edge.at[x + 2]
        return one.at[x - 1] if x < last else edge.at[x - last + 3]

    def twice(x):
        if x <= 1:
            return htwo.at[x + 1]
        return two.at[x - 2] if x < last - 1 else htwo.at[x - last + 4]

    def resid(x):
        if x <= 2:
            return redge.at[x]
        return rsd.at[x - 3] if x < last - 2 else redge.at[x - last + 5]

    return weights, scale, swept, twice, resid


def second_sweep(dims, nsrc, meta, cur, targets, weights, scale, swept, twice, regions):
    sweep(dims, swept, targets, weights, twice, regions=regions)
    sources(
        dims, meta, cur, nsrc, targets,
        lambda x, *rest: add_swept(twice(x), scale(x), *rest), regions,
    )


def residual(dims, nsrc, meta, cur, targets, weights, scale, twice, resid, regions):
    sweep(dims, twice, targets, weights, resid, scale, regions)

    def fix(x, col, h, amount):
        resid(x)[h, pl.ds(col, 1), :] += amount

    sources(dims, meta, cur, nsrc, targets, fix, regions)


def edge_kernel(dims, nsrc, meta, cur, table, xod, xev, wts, scl, one, two, res, vol, fx, fy, fz,
                hres, hvol, hfx, hfy, hfz, hwts, hscl, edge, htwo, redge):
    halves, cols = dims.halves, dims.cols
    odd_x = meta[3 * nsrc] == 1
    margin = PAD + HALO
    shuffle = depth_shuffle(dims.depth)
    for side in range(2):
        choose = lambda a, b: jnp.where(odd_x, b, a) if side == 0 else jnp.where(odd_x, a, b)
        for k in range(2):
            field = split_dot(choose(xod[k], xev[k]), shuffle)
            number = split_dot(choose(xod[2 + k], xev[2 + k]), shuffle, 1).astype(jnp.int32)
            inverse = jnp.where(number > 0, lookup(number - 1, table), 0.0)
            for h in range(halves):
                lanes = slice(h * LANES, (h + 1) * LANES)
                zero = jnp.zeros((margin, LANES), F32)
                for ref in (hres, hvol):
                    ref[2 * side + k, h, pl.ds(0, margin), :] = zero
                    ref[2 * side + k, h, pl.ds(margin + cols, margin), :] = zero
                wide = pl.ds(margin, cols)
                hvol[2 * side + k, h, wide, :] = field[:, lanes]
                hres[2 * side + k, h, wide, :] = inverse[:, lanes]
        for h in range(halves):
            hfy[side, h, pl.ds(PAD + dims.ext, PAD), :] = jnp.zeros((PAD, LANES), F32)
    edge_sweep(dims, nsrc, meta, cur, res, vol, fx, fy, fz, hres, hvol, hfx, hfy, hfz, hwts, hscl,
               edge, dims.inside, [(HALO, cols)])
    weights, scale, swept, twice, resid = edge_rows(
        dims, wts, scl, one, two, None, hwts, hscl, edge, htwo, redge
    )
    last = dims.rows - 1
    second_sweep(
        dims, nsrc, meta, cur, (0, 1, last - 1, last), weights, scale, swept, twice,
        dims.within(32),
    )
    residual(
        dims, nsrc, meta, cur, (1, 2, last - 2, last - 1), weights, scale, twice, resid,
        dims.within(40),
    )


def second_kernel(dims, nsrc, meta, cur, sod, sev, wts, scl, one, two, rsd, res, vol, fx, fy, fz,
                  ced, gci, ins, *refs):
    rows, halves, cols = dims.rows, dims.halves, dims.cols
    hres, hvol, hfx, hfy, hfz, hwts, hscl, edge, htwo, redge, gco, base, c_od, c_ev, v_od, v_ev = (
        refs[10:]
    )
    odd_x = meta[3 * nsrc] == 1
    last = rows - 1
    for side in range(2):
        choose = lambda a, b: jnp.where(odd_x, b, a) if side == 0 else jnp.where(odd_x, a, b)
        for h in range(halves):
            for k in range(2):
                for ref, kind in ((hvol, k), (hres, 2 + k)):
                    strip = halves * dims.ext + (kind * halves + h) * 2 * CORNER
                    low = pl.ds(strip, CORNER)
                    high = pl.ds(strip + CORNER, CORNER)
                    ref[2 * side + k, h, pl.ds(PAD + HALO - CORNER, CORNER), :] = choose(
                        sod[low, :], sev[low, :]
                    )
                    ref[2 * side + k, h, pl.ds(PAD + HALO + cols, CORNER), :] = choose(
                        sod[high, :], sev[high, :]
                    )
            span = pl.ds(h * dims.ext, dims.ext)
            edge[5 * side, h, pl.ds(PAD, dims.ext), :] = choose(sod[span, :], sev[span, :])
    edge_sweep(dims, nsrc, meta, cur, res, vol, fx, fy, fz, hres, hvol, hfx, hfy, hfz, hwts, hscl,
               edge, dims.strips, dims.strips)

    weights, scale, swept, twice, resid_row = edge_rows(
        dims, wts, scl, one, two, rsd, hwts, hscl, edge, htwo, redge
    )
    second_sweep(
        dims, nsrc, meta, cur, (0, 1, last - 1, last), weights, scale, swept, twice,
        dims.beside(32),
    )
    second_sweep(
        dims, nsrc, meta, cur, (-1, rows), weights, scale, swept, twice, dims.whole
    )
    pick_od = jnp.where(odd_x, 3, 2)
    pick_ev = jnp.where(odd_x, 2, 3)
    for h in range(halves):
        v_od[h, :, :] = htwo[pick_od, h, pl.ds(PAD, dims.ext), :]
        v_ev[h, :, :] = htwo[pick_ev, h, pl.ds(PAD, dims.ext), :]

    residual(
        dims, nsrc, meta, cur, (1, 2, last - 2, last - 1), weights, scale, twice, resid_row,
        dims.beside(40),
    )
    residual(
        dims, nsrc, meta, cur, (0, last), weights, scale, twice, resid_row, dims.whole
    )

    n = dims.crows
    bottom = restrict(dims, [hfx.at[1]], 0, (0, 1))
    topmost = restrict(dims, [hfx.at[2]], 0, (0, 1))

    e1, gc = [], []
    for c in range(n):
        total = restrict(dims, [resid_row(2 * c), resid_row(2 * c + 1)], 0, (0, 1))
        if 0 < c < n - 1:
            parts = [gci[k, c - 1] for k in range(7)]
        else:
            at = 0 if c == 0 else 4
            xl, xu = (bottom, ced[0]) if c == 0 else (ced[4], topmost)
            parts = coarse_weights(dims, ins[c], xl, xu, *(ced[at + k] for k in (1, 2, 3)))
            for k in range(6):
                gco[k, 0 if c == 0 else 1] = parts[k]
        gc.append(parts)
        e1.append(parts[6] * total)
        base[c] = e1[c]

    low = (e1[0], coarse_side(e1[0], e1[0], gc[0]) + gc[0][XU] * e1[1], gc[0][XL])
    high = (
        e1[n - 1],
        coarse_side(e1[n - 1], e1[n - 1], gc[n - 1]) + gc[n - 1][XL] * e1[n - 2],
        gc[n - 1][XU],
    )
    for k in range(3):
        c_od[k] = jnp.where(odd_x, high[k], low[k])
        c_ev[k] = jnp.where(odd_x, low[k], high[k])


def coarse_row(dims, gci, gco, c):
    if 0 < c < dims.crows - 1:
        return [gci[k, c - 1] for k in range(6)]
    return [gco[k, 0 if c == 0 else 1] for k in range(6)]


def third_kernel(dims, nsrc, meta, gci, gco, base, rod, rev, e3, c_od, c_ev):
    n = dims.crows
    odd_x = meta[3 * nsrc] == 1
    low = [jnp.where(odd_x, rev[k], rod[k]) for k in range(3)]
    high = [jnp.where(odd_x, rod[k], rev[k]) for k in range(3)]
    gc = lambda c: coarse_row(dims, gci, gco, c)

    def coarse_sweep(field, under, over):
        out = []
        for c in range(n):
            w = gc(c)
            new = coarse_side(field[c], base[c], w)
            new += w[XL] * (field[c - 1] if c else under)
            new += w[XU] * (field[c + 1] if c < n - 1 else over)
            out.append(new)
        return out

    e1 = [base[c] for c in range(n)]
    e2 = coarse_sweep(e1, low[0], high[0])
    under = low[1] + low[2] * e1[0]
    over = high[1] + high[2] * e1[n - 1]
    out = coarse_sweep(e2, under, over)
    for c in range(n):
        e3[c] = out[c]
    w = gc(0)
    first = (out[0], coarse_side(out[0], base[0], w) + w[XU] * out[1])
    w = gc(n - 1)
    final = (out[n - 1], coarse_side(out[n - 1], base[n - 1], w) + w[XL] * out[n - 2])
    for k in range(2):
        c_od[k] = jnp.where(odd_x, final[k], first[k])
        c_ev[k] = jnp.where(odd_x, first[k], final[k])


def fourth_kernel(dims, nsrc, meta, cur, gci, gco, base, e3, rod, rev, tod, tev, vod, vev, wts, scl,
                  two, hwts, hscl, htwo, out, raised, zero, three, done, sems):
    rows, halves, cols = dims.rows, dims.halves, dims.cols
    n = dims.crows
    odd_x = meta[3 * nsrc] == 1
    below_of = lambda od, ev: jnp.where(odd_x, ev, od)
    above_of = lambda od, ev: jnp.where(odd_x, od, ev)
    field = [e3[c] for c in range(n)]
    under = below_of(tod[1], tev[1]) + below_of(rod[2], rev[2]) * field[0]
    over = above_of(tod[1], tev[1]) + above_of(rod[2], rev[2]) * field[n - 1]
    e4 = [under]
    for c in range(n):
        w = coarse_row(dims, gci, gco, c)
        new = coarse_side(field[c], base[c], w)
        new += w[XL] * (field[c - 1] if c else below_of(tod[0], tev[0]))
        new += w[XU] * (field[c + 1] if c < n - 1 else above_of(tod[0], tev[0]))
        e4.append(new)
    e4.append(over)
    for c in range(n + 2):
        raised[c, pl.ds(0, dims.cext, stride=2), :] = e4[c]
        raised[c, pl.ds(1, dims.cext, stride=2), :] = e4[c]

    last = rows - 1

    def twice(x):
        if x <= 1:
            return htwo.at[x + 1]
        return two.at[x - 2] if x < last - 1 else htwo.at[x - last + 4]

    outer = lambda x: x + 1 if x <= 0 else x - last + 2
    inner = lambda x: 1 <= x <= last - 1
    weights = lambda x: [
        wts.at[k, x - 1] if inner(x) else hwts.at[k, outer(x)] for k in range(6)
    ]
    scale = lambda x: scl.at[x - 1] if inner(x) else hscl.at[outer(x)]
    for x in range(-2, rows + 2):
        for h in range(halves):
            near = pl.ds(TRIM, dims.ext - 2 * TRIM)
            wide = pl.ds(PAD + TRIM, dims.ext - 2 * TRIM)
            if x == -2:
                value = below_of(vod[h, near, :], vev[h, near, :])
            elif x == rows + 1:
                value = above_of(vod[h, near, :], vev[h, near, :])
            else:
                value = twice(x)[h, wide, :]
            zero[x + 2, h, wide, :] = value + raised[(x + 2) // 2, near, :]
    sweep(
        dims, lambda x: zero.at[x + 2], range(-1, rows + 1), weights, lambda x: three.at[x + 1],
        regions=dims.within(TRIM),
    )
    sources(
        dims, meta, cur, nsrc, range(-1, rows + 1),
        lambda x, *rest: add_swept(three.at[x + 1], scale(x), *rest), dims.within(TRIM),
    )
    copies = []
    shuffle = depth_shuffle(dims.depth, True)
    groups = [range(at, min(at + GROUP, rows)) for at in range(0, rows, GROUP)]
    inside = pl.ds(PAD + HALO, cols)
    four = lambda x: zero.at[x + 2]
    for k, group in enumerate(groups + [()]):
        if k:
            for x in groups[k - 1]:
                field = jnp.concatenate([four(x)[h, inside, :] for h in range(halves)], axis=1)
                done[x] = split_dot(field, shuffle)
        if group:
            sweep(
                dims, lambda x: three.at[x + 1], group, weights, four, regions=[(HALO, cols)]
            )
        if k:
            for x in groups[k - 1]:
                copy = pltpu.make_async_copy(done.at[x], out.at[x], sems.at[x])
                copy.start()
                copies.append(copy)
        if group:
            sources(
                dims, meta, cur, nsrc, group,
                lambda x, *rest: add_swept(four(x), scale(x), *rest), [(HALO, cols)],
            )
    for copy in copies:
        copy.wait()


def call(kernel, outs, ins, specs, scratch=(), aliases=None, out_specs=None, limit=24, cost=1):
    return pl.pallas_call(
        kernel,
        out_shape=[jax.ShapeDtypeStruct(shape, F32) for shape in outs],
        in_specs=specs,
        out_specs=out_specs if out_specs is not None else [VM] * len(outs),
        scratch_shapes=list(scratch),
        input_output_aliases=aliases or {},
        compiler_params=pltpu.CompilerParams(vmem_limit_bytes=limit * 2**20),
        cost_estimate=pl.CostEstimate(flops=cost, bytes_accessed=cost, transcendentals=0),
    )(*ins)


def swaps(count):
    pairs = []
    for first in (1, 0):
        found = []
        for low in range(first, count - 1, 2):
            found += [(low, low + 1), (low + 1, low)]
        pairs.append(found)
    return pairs


def swap(od, ev, axis):
    odd_pairs, even_pairs = swaps(lax.axis_size(axis))
    return lax.ppermute(od, axis, odd_pairs), lax.ppermute(ev, axis, even_pairs)


def per_device(potential, classes, sigma_table, row_index, col_index, depth_index, currents):
    dims = Dims(potential.shape)
    rows, cols, depth = potential.shape
    halves, ext, padded, n, cext = dims.halves, dims.ext, dims.padded, dims.crows, dims.cext
    nsrc = row_index.shape[0]
    gx, gy = lax.axis_index("gx"), lax.axis_index("gy")
    odd_x, odd_y = gx % 2, gy % 2
    meta = jnp.concatenate(
        [
            row_index - gx * rows,
            col_index - gy * cols,
            depth_index,
            jnp.stack([odd_x, odd_y]),
        ]
    ).astype(jnp.int32)
    table = 1.0 / sigma_table

    bind = lambda kernel: functools.partial(kernel, dims, nsrc)
    wide = lambda k: (k, halves, padded, LANES)
    flat = lambda k: (k, halves, ext, LANES)
    send = (halves * ext + 4 * halves * 2 * CORNER, LANES)
    coarse = lambda *k: (*k, cext, LANES)
    vmem = lambda *shapes: [pltpu.VMEM(shape, F32) for shape in shapes]
    hbm = pl.BlockSpec(memory_space=pl.ANY)
    far = pl.BlockSpec(memory_space=pltpu.HBM)

    def edge(axis, dim, width, wanted, shape, kept):
        (out,) = call(
            functools.partial(edge_message, axis, dim, width, wanted), [shape],
            [potential, classes], [far] * 2,
            scratch=[pltpu.VMEM(kept, jnp.int32), pltpu.SemaphoreType.DMA((2,))],
            limit=54,
        )
        return out

    xod, xev = swap(
        *(edge("gx", 0, 2, k, (4, cols, depth), (2, cols, depth)) for k in (1, 0)), "gx"
    )
    yod, yev = swap(
        *(
            edge("gy", 1, HALO, k, (2, rows, HALO, depth), (rows, HALO, depth))
            for k in (1, 0)
        ),
        "gy",
    )
    tile = dims.tile = [
        wide(4), wide(4), flat(2), wide(2), flat(2), wide(rows - 4), wide(rows - 4),
        flat(rows - 3), wide(rows - 2), flat(rows - 2), (6, *flat(rows - 2)), flat(rows - 2),
        wide(rows - 2),
    ]
    parts = call(
        bind(tile_kernel), tile, [meta, currents, table, potential, classes],
        [SM] * 3 + [VM] * 2,
        limit=4,
    )
    parts = call(
        bind(strip_kernel),
        tile + [send, send],
        [meta, currents, table, yod, yev, *parts],
        [SM] * 3 + [VM] * (2 + len(tile)),
        aliases={5 + k: k for k in range(len(tile))},
        limit=4,
    )
    res, vol, fx, fy, fz = parts[:5]
    wts, scl, one, s_od, s_ev = parts[10:]
    sod, sev = swap(s_od, s_ev, "gx")
    (two, rsd, ced, gci, ins) = call(
        bind(first_kernel),
        [wide(rows - 4), flat(rows - 6), coarse(8), coarse(7, n - 2), coarse(n)],
        [meta, currents, *parts[: len(tile) + 1]],
        [SM] * 2 + [VM] * (len(tile) + 1),
        scratch=vmem(coarse(4 * n + 1)),
        limit=4,
    )
    held = [
        wide(4), wide(4), flat(4), wide(2), flat(2), (6, *flat(4)), flat(4), wide(6), wide(6),
        flat(6),
    ]
    edges = call(
        bind(edge_kernel),
        held,
        [meta, currents, table, xod, xev, wts, scl, one, two, res, vol, fx, fy, fz],
        [SM] * 3 + [VM] * 11,
        limit=3,
    )
    ins_of = [meta, currents, sod, sev, wts, scl, one, two, rsd, res, vol, fx, fy, fz, ced, gci, ins]
    outs = call(
        bind(second_kernel),
        held + [coarse(6, 2), coarse(n), coarse(3), coarse(3)] + [flat(1)[1:]] * 2,
        ins_of + list(edges),
        [SM] * 2 + [VM] * (len(ins_of) - 2 + len(held)),
        aliases={len(ins_of) + k: k for k in range(len(held))},
        limit=4,
    )
    hwts, hscl, htwo = outs[5], outs[6], outs[8]
    gco, base, c_od, c_ev, v_od, v_ev = outs[10:]
    rod, rev = swap(c_od, c_ev, "gx")
    vod, vev = swap(v_od, v_ev, "gx")
    (e3, t_od, t_ev) = call(
        bind(third_kernel),
        [coarse(n), coarse(2), coarse(2)],
        [meta, gci, gco, base, rod, rev],
        [SM] + [VM] * 5,
        limit=4,
    )
    tod, tev = swap(t_od, t_ev, "gx")
    (out,) = call(
        bind(fourth_kernel),
        [(rows, cols, depth)],
        [meta, currents, gci, gco, base, e3, rod, rev, tod, tev, vod, vev, wts, scl, two, hwts,
         hscl, htwo],
        [SM] * 2 + [VM] * 16,
        scratch=vmem((n + 2, ext, LANES), wide(rows + 4), wide(rows + 2),
                     (rows, cols, depth))
        + [pltpu.SemaphoreType.DMA((rows,))],
        out_specs=[hbm],
        limit=13,
    )
    return out


def solution(mesh):
    tiled = P("gx", "gy", None)
    return jax.shard_map(
        per_device,
        mesh=mesh,
        in_specs=(tiled, tiled, P(), P(), P(), P(), P()),
        out_specs=tiled,
        check_vma=False,
    )
```
